128 devices in a mesh: dp: 8 (over z, x_hi), tensor: 16 (over y, x_lo, core).
Axes of the slice: x: 4 (x_hi: 2, x_lo: 2; x = x_hi * 2 + x_lo), y: 4, z: 4, core: 2. Of those that a mesh axis runs over, the one named last changes fastest.
Arguments:
- tokens: bfloat16 [4096, 8192], P('dp', 'tensor'), may hold values from -6 to 6
- frozen: bfloat16 [8192, 8192], P('tensor'), may hold values from -0.0625 to 0.0625
- local_param: float32 [64, 128, 128], P('tensor'), may hold values from -0.2 to 0.2
- cross_param: float32 [4, 64, 128, 128], P(None, 'tensor'), may hold values from -0.2 to 0.2
- out_grad: bfloat16 [4096, 8192], P('dp', 'tensor'), may hold values from -0.09375 to 0.09375
Outputs:
- output: float32 [4096, 8192], P('dp', 'tensor')
- local_grad: float32 [64, 128, 128], P('tensor')
- cross_grad: float32 [4, 64, 128, 128], P(None, 'tensor')
The draws below stay inside these ranges and needn't reach their ends.
All inputs are finite; a program needn't handle non-finite values.
Results may differ from the reference program's by a relative error of at most 0.0029.
Values may be sent and summed in bfloat16 or wider, within the bound.
A program may use at most 192 MiB of HBM per device.

```python
import jax
import jax.numpy as jnp
from jax import lax

D = 8192
BLOCK = 128
LEVELS = 4
TOKENS = 4096
N_TENSOR = 16


def block_levels(own_key, shape, shards, low, top_value):
    gain = 1.0
    for axis_at, shards_of in shards:
        draws = jax.random.uniform(jax.random.fold_in(jax.random.fold_in(own_key, 6), axis_at), (shards_of,), jnp.float32, low / len(shards), top_value / len(shards))
        gain = gain * jnp.repeat(jnp.exp(draws), shape[axis_at] // shards_of).reshape((-1,) + (1,) * (len(shape) - 1 - axis_at))
    return gain


def normal_values(stream_key, dims, scale, reach, shards=(), held_as=jnp.bfloat16):
    drawn = scale * jax.random.normal(stream_key, dims, jnp.float32)
    if shards:
        drawn = drawn * block_levels(stream_key, dims, shards, -0.22, 0.18)
    return jnp.clip(drawn, -reach, reach).astype(held_as)


def setup_inputs(seed: int = 0) -> dict:
    seeds = jax.random.split(jax.random.key(seed), 6)
    return {
        "tokens": normal_values(seeds[0], (TOKENS, D), 1.0, 6.0, ((0, 8), (1, 16))),
        "frozen": normal_values(seeds[1], (D, D), D ** -0.5, 0.0625, ((0, 16),)),
        "local_param": normal_values(seeds[2], (D // BLOCK, BLOCK, BLOCK), 0.03, 0.2, ((0, 16),), jnp.float32),
        "cross_param": normal_values(seeds[3], (LEVELS, D // BLOCK, BLOCK, BLOCK), 0.03, 0.2, ((1, 16),), jnp.float32),
        "out_grad": normal_values(seeds[4], (TOKENS, D), (TOKENS ** -0.5), 0.09375, ((0, 8), (1, 16))),
    }


def cayley_block(param):
    highest = lax.Precision.HIGHEST
    skew = param - param.T
    identity = jnp.eye(param.shape[0], dtype=param.dtype)
    one_minus = identity - skew
    spd_matrix = identity - jnp.dot(skew, skew, precision=highest)
    numerator = jnp.dot(one_minus, one_minus, precision=highest)
    chol_factor = jnp.linalg.cholesky(spd_matrix)
    return jax.scipy.linalg.cho_solve((chol_factor, True), numerator.T).T

def cayley_many(params):
    return jax.vmap(cayley_block)(params)

def rotate(inputs, local_param, cross_param):
    highest = lax.Precision.HIGHEST
    token_count = inputs.shape[0]
    blocks_dev = D // N_TENSOR // BLOCK
    half_block = BLOCK // 2
    local_rot = cayley_many(local_param).reshape(N_TENSOR, blocks_dev, BLOCK, BLOCK)
    state = inputs.reshape(token_count, N_TENSOR, blocks_dev, BLOCK)
    state = jnp.einsum('tnci,ncij->tncj', state, local_rot, precision=highest).reshape(token_count, D)
    for level_idx in range(LEVELS):
        stride_dev = 2 ** level_idx
        outer_pairs = N_TENSOR // (2 * stride_dev)
        cross_rot = cayley_many(cross_param[level_idx]).reshape(outer_pairs, 2, stride_dev, blocks_dev, BLOCK, BLOCK)
        cross_rot = cross_rot.transpose(0, 2, 1, 3, 4, 5).reshape(outer_pairs, stride_dev, 2 * blocks_dev, BLOCK, BLOCK)
        grouped = state.reshape(token_count, outer_pairs, 2, stride_dev, 2 * blocks_dev, half_block)
        grouped = grouped.transpose(0, 1, 3, 4, 2, 5).reshape(token_count, outer_pairs, stride_dev, 2 * blocks_dev, BLOCK)
        mixed = jnp.einsum('tabgi,abgij->tabgj', grouped, cross_rot, precision=highest)
        mixed = mixed.reshape(token_count, outer_pairs, stride_dev, 2 * blocks_dev, 2, half_block)
        state = mixed.transpose(0, 1, 4, 2, 3, 5).reshape(token_count, D)
    return state

def reference(tokens, frozen, local_param, cross_param, out_grad):
    inputs = tokens.astype(jnp.float32)

    def apply_factors(first_param, second_param):
        return rotate(inputs, first_param, second_param)
    rotated, pullback = jax.vjp(apply_factors, local_param, cross_param)
    rounded = rotated.astype(jnp.bfloat16)
    output = jnp.dot(rounded.astype(jnp.float32), frozen.astype(jnp.float32), preferred_element_type=jnp.float32)
    rotated_grad = jnp.dot(out_grad.astype(jnp.float32), frozen.T.astype(jnp.float32), preferred_element_type=jnp.float32)
    local_grad, cross_grad = pullback(rotated_grad)
    return (output, local_grad, cross_grad)
```

```python
import jax
import jax.numpy as jnp
from jax import lax
from jax.experimental import pallas as pl
from jax.experimental.pallas import tpu as pltpu
from jax.sharding import PartitionSpec as P


def from_partner(shard, axis, stride):
    return lax.ppermute(shard, axis, [(i, i ^ 1 << stride) for i in range(lax.axis_size(axis))])


def inverse_kernel(param_ref, out_ref):
    count, size, _ = param_ref.shape
    rows = lax.broadcasted_iota(jnp.int32, (size, size), 0)
    lanes = lax.broadcasted_iota(jnp.int32, (size, size), 1)
    row_lanes = lax.broadcasted_iota(jnp.int32, (1, size), 1)
    identity = jnp.where(rows == lanes, 1.0, 0.0)
    for at in range(count):
        param = param_ref[at]
        out_ref[at] = identity + param - param.T

    def eliminate(k, carry):
        for at in range(count):
            matrix = out_ref[at]
            row = out_ref[at, pl.ds(k, 1), :]
            hit = lanes == k
            column = jnp.sum(jnp.where(hit, matrix, 0.0), axis=1, keepdims=True)
            pivot = jnp.sum(jnp.where(row_lanes == k, row, 0.0), axis=1, keepdims=True)
            scale = 1.0 / pivot
            new_row = jnp.where(row_lanes == k, scale, row * scale)
            out_ref[at] = jnp.where(hit, 0.0, matrix) - column * new_row
            out_ref[at, pl.ds(k, 1), :] = new_row
        return carry

    lax.fori_loop(0, size, eliminate, 0)


def inverse_many(params):
    return pl.pallas_call(
        inverse_kernel,
        out_shape=jax.ShapeDtypeStruct(params.shape, jnp.float32),
        compiler_params=pltpu.CompilerParams(vmem_limit_bytes=32 << 20),
    )(params)


def pull_many(inverse, matrix_grad):
    highest = lax.Precision.HIGHEST
    left = jnp.einsum("nji,njk->nik", inverse, matrix_grad, precision=highest)
    full = jnp.einsum("nik,njk->nij", left, inverse, precision=highest)
    return -2.0 * (full - full.transpose(0, 2, 1))


def split_halves(state, upper_side, blocks_dev, half_block):
    halves = state.reshape(state.shape[0], 2, blocks_dev, half_block)
    own_part = jnp.where(upper_side, halves[:, 1], halves[:, 0])
    other_part = jnp.where(upper_side, halves[:, 0], halves[:, 1])
    return (own_part, other_part)


def join_pair(own_part, received, upper_side):
    low_half = jnp.where(upper_side, received, own_part)
    high_half = jnp.where(upper_side, own_part, received)
    return jnp.concatenate([low_half, high_half], axis=-1)


def split_pair(vector, upper_side, half_block):
    low_half = vector[..., :half_block]
    high_half = vector[..., half_block:]
    keep_part = jnp.where(upper_side, high_half, low_half)
    give_part = jnp.where(upper_side, low_half, high_half)
    return (keep_part, give_part)


def merge_halves(keep_part, returned, upper_side):
    first_half = jnp.where(upper_side, returned, keep_part)
    second_half = jnp.where(upper_side, keep_part, returned)
    return jnp.stack([first_half, second_half], axis=1).reshape(keep_part.shape[0], -1)


def sum_data(value):
    return lax.psum(value, "dp")


def body(tokens, frozen, local_param, cross_param, out_grad):
    highest = lax.Precision.HIGHEST
    token_count, rows_dev = tokens.shape
    block = local_param.shape[-1]
    half_block = block // 2
    blocks_dev = local_param.shape[0]
    levels = lax.axis_size("tensor").bit_length() - 1
    position = lax.axis_index("tensor")
    params = jnp.concatenate([local_param, cross_param.reshape(-1, block, block)])
    inverse = inverse_many(params)
    rotations = 2.0 * inverse - jnp.eye(block, dtype=jnp.float32)
    local_rot = rotations[:blocks_dev]
    cross_rot = rotations[blocks_dev:].reshape(levels, blocks_dev, block, block)
    inputs = tokens.astype(jnp.float32).reshape(token_count, blocks_dev, block)
    state = jnp.einsum("tci,cij->tcj", inputs, local_rot, precision=highest).reshape(
        token_count, rows_dev
    )
    saved = []
    for level_idx in range(levels):
        upper_side = position >> level_idx & 1 == 1
        own_part, other_part = split_halves(state, upper_side, blocks_dev, half_block)
        received = from_partner(other_part, "tensor", level_idx)
        vector = join_pair(own_part, received, upper_side)
        mixed = jnp.einsum("tci,cij->tcj", vector, cross_rot[level_idx], precision=highest)
        keep_part, give_part = split_pair(mixed, upper_side, half_block)
        returned = from_partner(give_part, "tensor", level_idx)
        state = merge_halves(keep_part, returned, upper_side)
        saved.append(vector)
    rounded = state.astype(jnp.bfloat16)
    partial_out = jnp.dot(rounded, frozen, preferred_element_type=jnp.float32)
    output = lax.psum_scatter(partial_out, "tensor", scatter_dimension=1, tiled=True)
    grad_state = lax.dot_general(
        lax.all_gather(out_grad, "tensor", axis=1, tiled=True),
        frozen,
        (((1,), (1,)), ((), ())),
        preferred_element_type=jnp.float32,
    )
    cross_grads = [None] * levels
    for level_idx in reversed(range(levels)):
        upper_side = position >> level_idx & 1 == 1
        own_part, other_part = split_halves(grad_state, upper_side, blocks_dev, half_block)
        received = from_partner(other_part, "tensor", level_idx)
        grad_vector = join_pair(own_part, received, upper_side)
        matrix_grad = jnp.einsum("tci,tcj->cij", saved[level_idx], grad_vector, precision=highest)
        back_vector = jnp.einsum(
            "tcj,cij->tci", grad_vector, cross_rot[level_idx], precision=highest
        )
        keep_part, give_part = split_pair(back_vector, upper_side, half_block)
        returned = from_partner(give_part, "tensor", level_idx)
        grad_state = merge_halves(keep_part, returned, upper_side)
        cross_grads[level_idx] = matrix_grad
    grad_blocks = grad_state.reshape(token_count, blocks_dev, block)
    local_matrix = jnp.einsum("tci,tcj->cij", inputs, grad_blocks, precision=highest)
    grads = pull_many(inverse, sum_data(jnp.concatenate([local_matrix] + cross_grads)))
    local_grad = grads[:blocks_dev]
    cross_grad = grads[blocks_dev:].reshape(levels, blocks_dev, block, block)
    return (output, local_grad, cross_grad)


def solution(mesh):
    in_specs = (
        P("dp", "tensor"),
        P("tensor", None),
        P("tensor", None, None),
        P(None, "tensor", None, None),
        P("dp", "tensor"),
    )
    out_specs = (P("dp", "tensor"), P("tensor", None, None), P(None, "tensor", None, None))
    return jax.shard_map(body, mesh=mesh, in_specs=in_specs, out_specs=out_specs, check_vma=False)
```

```python
import functools

import jax
import jax.numpy as jnp
from jax import lax
from jax.experimental import pallas as pl
from jax.experimental.pallas import tpu as pltpu
from jax.sharding import PartitionSpec as P

MESH = pl.DeviceIdType.MESH
F32 = jnp.float32
BF16 = jnp.bfloat16
ANY = pl.BlockSpec(memory_space=pl.ANY)
VMEM = pl.BlockSpec(memory_space=pltpu.VMEM)
DMA = pltpu.SemaphoreType.DMA
GROUP = 16
CHIPS = 8
HALF = 64
BLOCK = 128
ROWS = 256


def params_of(identity, vmem=60):
    return pltpu.CompilerParams(
        collective_id=identity, has_side_effects=True, vmem_limit_bytes=vmem << 20
    )


def meet(peers):
    barrier = pltpu.get_barrier_semaphore()
    for peer in peers:
        pl.semaphore_signal(barrier, inc=1, device_id={"tensor": peer}, device_id_type=MESH)
    pl.semaphore_wait(barrier, len(peers))


def push(src, dst, send, recv, peer):
    return pltpu.make_async_remote_copy(
        src_ref=src, dst_ref=dst, send_sem=send, recv_sem=recv,
        device_id={"tensor": peer}, device_id_type=MESH,
    )


def arrived(ref, sem):
    pltpu.make_async_copy(ref, ref, sem).wait()


def split(value):
    high = value.astype(BF16)
    return high, (value - high.astype(F32)).astype(BF16)


def dot(a, b, dims=(((1,), (0,)), ((), ()))):
    return lax.dot_general(a, b, dims, preferred_element_type=F32)


NT = (((1,), (1,)), ((), ()))
TN = (((0,), (0,)), ((), ()))


def dot3(a, b, dims=(((1,), (0,)), ((), ()))):
    return dot(a[0], b[0], dims) + (dot(a[0], b[1], dims) + dot(a[1], b[0], dims))


def spread_kernel(tok_ref, froz_ref, x_ref, cat_ref, tsend, trecv, fsend, frecv, local, flocal):
    me = lax.axis_index("tensor")
    core = lax.rem(me, 2)
    partner = me + 1 - 2 * core
    others = [lax.rem(me + k, GROUP) for k in range(1, GROUP)]
    meet(others)

    def token_slice(peer):
        column = pl.multiple_of((peer // 4) * BLOCK, BLOCK)
        row = pl.multiple_of(lax.rem(peer, 2) * ROWS, ROWS)
        return tok_ref.at[pl.ds(row, ROWS), pl.ds(column, BLOCK)]

    sends = []
    for k, peer in enumerate(others):
        copy = push(token_slice(peer), x_ref.at[me], tsend.at[k], trecv.at[me], peer)
        copy.start()
        sends.append(copy)
    for j in range(CHIPS):
        theirs = pl.multiple_of((2 * j + 1 - core) * 512, 512)
        copy = push(
            froz_ref.at[:, :, pl.ds(theirs, 512)], cat_ref.at[:, core, :, pl.ds(j * 512, 512)],
            fsend.at[j], frecv.at[j], partner,
        )
        copy.start()
        sends.append(copy)
    own = pltpu.make_async_copy(token_slice(me), x_ref.at[me], local)
    own.start()
    keeps = []
    for j in range(CHIPS):
        mine = pl.multiple_of((2 * j + core) * 512, 512)
        copy = pltpu.make_async_copy(
            froz_ref.at[:, :, pl.ds(mine, 512)], cat_ref.at[:, core, :, pl.ds(j * 512, 512)],
            flocal.at[j],
        )
        copy.start()
        keeps.append(copy)
    own.wait()
    for copy in keeps:
        copy.wait()
    for copy in sends:
        copy.wait_send()
    for peer in others:
        arrived(x_ref.at[peer], trecv.at[peer])
    for j in range(CHIPS):
        arrived(cat_ref.at[:, 1 - core, :, pl.ds(j * 512, 512)], frecv.at[j])


def spread(tokens, frozen):
    return pl.pallas_call(
        spread_kernel,
        out_shape=(
            jax.ShapeDtypeStruct((GROUP, ROWS, BLOCK), BF16),
            jax.ShapeDtypeStruct((CHIPS, 2, HALF, 4096), BF16),
        ),
        in_specs=[ANY, ANY],
        out_specs=(ANY, ANY),
        scratch_shapes=[
            DMA((GROUP,)), DMA((GROUP,)), DMA((CHIPS,)), DMA((CHIPS,)), DMA, DMA((CHIPS,)),
        ],
        compiler_params=params_of(0),
    )(tokens, frozen.reshape(CHIPS, HALF, 8192))


def inverse_kernel(param_ref, out_ref, rot_ref):
    count, size, _ = param_ref.shape
    step = 32
    rows = lax.broadcasted_iota(jnp.int32, (size, size), 0)
    lanes = lax.broadcasted_iota(jnp.int32, (size, size), 1)
    panel_rows = lax.broadcasted_iota(jnp.int32, (step, size), 0)
    panel_lanes = lax.broadcasted_iota(jnp.int32, (step, size), 1)
    identity = jnp.where(rows == lanes, 1.0, 0.0)
    for at in range(count):
        param = param_ref[at]
        out_ref[at] = identity + param - param.T

    def eliminate(block_at, carry):
        start = pl.multiple_of(block_at * step, step)
        shift = lax.rem(size - start, size)
        inside = (lanes >= start) & (lanes < start + step)
        panels = [pltpu.roll(out_ref[at, pl.ds(start, step), :], shift, 1) for at in range(count)]
        for k in range(step):
            for at in range(count):
                panel = panels[at]
                column = panel[:, k:k + 1]
                scale = 1.0 / panel[k:k + 1, k:k + 1]
                row = jnp.where(panel_lanes[:1] == k, 1.0, panel[k:k + 1, :]) * scale
                rest = jnp.where(panel_lanes == k, 0.0, panel) - column * row
                panels[at] = jnp.where(panel_rows == k, row, rest)
        panels = [pltpu.roll(panel, start, 1) for panel in panels]
        for at in range(count):
            matrix = out_ref[at]
            turned = pltpu.roll(matrix, shift, 1)[:, :step]
            out_ref[at] = jnp.where(inside, 0.0, matrix) - jnp.dot(
                turned, panels[at], precision=lax.Precision.HIGHEST, preferred_element_type=F32
            )
        for at in range(count):
            out_ref[at, pl.ds(start, step), :] = panels[at]
        return carry

    lax.fori_loop(0, size // step, eliminate, 0)
    for at in range(count):
        rotation = 2.0 * out_ref[at] - identity
        rot_ref[at] = rotation.T if at < 4 else rotation


def inverse_many(params):
    shape = jax.ShapeDtypeStruct(params.shape, F32)
    return pl.pallas_call(
        inverse_kernel,
        out_shape=(shape, shape),
        compiler_params=pltpu.CompilerParams(vmem_limit_bytes=32 << 20),
    )(params)


def pair_place(me, level):
    low = 2 ** level
    bit = lax.rem(me // low, 2)
    pair = (me // (2 * low)) * low + lax.rem(me, low)
    return bit, pair


def pair_owner(pair, level, bit):
    low = 2 ** level
    return (pair // low) * (2 * low) + bit * low + lax.rem(pair, low)


def route_kernel(rot_ref, cross_ref, local_ref, send, recv, lsend, lrecv, fsend, frecv):
    me = lax.axis_index("tensor")
    core = lax.rem(me, 2)
    chip = me // 2
    partner = me + 1 - 2 * core
    meet([lax.rem(me + k, GROUP) for k in range(1, GROUP)])

    def start(src, dst, send_sem, recv_sem, peer):
        @pl.when(peer == me)
        def _():
            pltpu.make_async_copy(src, dst, recv_sem).start()

        @pl.when(peer != me)
        def _():
            push(src, dst, send_sem, recv_sem, peer).start()

    def drain(src, dst, send_sem, recv_sem, peer):
        @pl.when(peer != me)
        def _():
            push(src, dst, send_sem, recv_sem, peer).wait_send()

    jobs = []
    for level in range(4):
        bit, pair = pair_place(me, level)
        for c in range(4):
            peer = 2 * (c + 4 * bit) + lax.rem(pair, 2)
            jobs.append((
                rot_ref.at[4 + 4 * level + c], cross_ref.at[level, pair // 2, lax.rem(pair, 2)],
                send.at[level, c], recv.at[level, pair // 2], peer,
            ))
    for c in range(4):
        for side in range(2):
            peer = 2 * (2 * c + side) + core
            jobs.append((
                rot_ref.at[c, pl.ds(side * HALF, HALF), :], local_ref.at[chip, core],
                lsend.at[c, side], lrecv.at[chip], peer,
            ))
    for job in jobs:
        start(*job)
    forwards = []
    for level in range(4):
        for q in range(4):
            arrived(cross_ref.at[level, q, core], recv.at[level, q])
        part = cross_ref.at[level, :, core]
        copy = push(part, part, fsend.at[level], frecv.at[level], partner)
        copy.start()
        forwards.append(copy)
    for q in range(CHIPS):
        arrived(local_ref.at[q, core], lrecv.at[q])
    part = local_ref.at[:, core]
    copy = push(part, part, fsend.at[4], frecv.at[4], partner)
    copy.start()
    forwards.append(copy)
    for job in jobs:
        drain(*job)
    for copy in forwards:
        copy.wait_send()
    for level in range(4):
        arrived(cross_ref.at[level, :, 1 - core], frecv.at[level])
    arrived(local_ref.at[:, 1 - core], frecv.at[4])


def route(rotations):
    return pl.pallas_call(
        route_kernel,
        out_shape=(
            jax.ShapeDtypeStruct((4, 4, 2, BLOCK, BLOCK), F32),
            jax.ShapeDtypeStruct((CHIPS, 2, HALF, BLOCK), F32),
        ),
        in_specs=[ANY],
        out_specs=(ANY, ANY),
        scratch_shapes=[
            DMA((4, 4)), DMA((4, 4)), DMA((4, 2)), DMA((CHIPS,)), DMA((5,)), DMA((5,)),
        ],
        compiler_params=params_of(1),
    )(rotations)


def mix(a, b, r):
    at = (r // 2) * BLOCK
    first, second = a[:, at:at + BLOCK], b[:, at:at + BLOCK]
    lanes = lax.broadcasted_iota(jnp.int32, first.shape, 1)
    if r % 2 == 0:
        return jnp.where(lanes < HALF, first, pltpu.roll(second, HALF, 1))
    return jnp.where(lanes < HALF, pltpu.roll(first, HALF, 1), second)


def regroup(quads):
    return [
        jnp.concatenate([mix(quads[0], quads[1], r), mix(quads[2], quads[3], r)], axis=1)
        for r in range(4)
    ]


def place_near(a, b):
    zero = jnp.zeros((BLOCK, BLOCK), F32)
    return jnp.concatenate(
        [jnp.concatenate([a, zero], axis=1), jnp.concatenate([zero, b], axis=1)], axis=0
    )


def place_far(a, b):
    lanes = lax.broadcasted_iota(jnp.int32, (BLOCK, BLOCK), 1)
    turned_a, turned_b = pltpu.roll(a, HALF, 1), pltpu.roll(b, HALF, 1)
    low = lanes < HALF
    a_rows = jnp.concatenate([jnp.where(low, a, 0.0), jnp.where(low, turned_a, 0.0)], axis=1)
    b_rows = jnp.concatenate([jnp.where(low, 0.0, turned_b), jnp.where(low, 0.0, b)], axis=1)
    return jnp.concatenate(
        [a_rows[:HALF], b_rows[:HALF], a_rows[HALF:], b_rows[HALF:]], axis=0
    )


def take_far(full):
    lanes = lax.broadcasted_iota(jnp.int32, (BLOCK, BLOCK), 1)
    low = lanes < HALF
    a_rows = jnp.concatenate([full[:HALF], full[BLOCK:BLOCK + HALF]], axis=0)
    b_rows = jnp.concatenate([full[HALF:BLOCK], full[BLOCK + HALF:]], axis=0)
    a = jnp.where(low, a_rows[:, :BLOCK], pltpu.roll(a_rows[:, BLOCK:], HALF, 1))
    b = jnp.where(low, pltpu.roll(b_rows[:, :BLOCK], HALF, 1), b_rows[:, BLOCK:])
    return a, b


def pairs_of(level, index):
    if level < 2:
        return 2 * index, 2 * index + 1
    return index, 4 + index


def forward_kernel(
    x_ref, cross_ref, local_ref, mats_ref, saved_ref, act_ref, rot_scr, send, recv, local, fsend, frecv
):
    me = lax.axis_index("tensor")
    core = lax.rem(me, 2)
    chip = me // 2
    partner = me + 1 - 2 * core
    peers = [lax.rem(me + 2 * k, GROUP) for k in range(1, CHIPS)]
    meet(peers + [partner])
    for level in range(4):
        for index in range(4):
            one, two = pairs_of(level, index)
            a = cross_ref[level, one // 2, one % 2]
            b = cross_ref[level, two // 2, two % 2]
            full = place_near(a, b) if level % 2 == 0 else place_far(a, b)
            high, low = split(full)
            mats_ref[level, index, 0] = high
            mats_ref[level, index, 1] = low
    lanes = lax.broadcasted_iota(jnp.int32, (ROWS, BLOCK), 1)
    for m in range(CHIPS):
        parts = []
        for side in range(2):
            high, low = split(jnp.concatenate([local_ref[m, side]] * 2, axis=0))
            x = x_ref[2 * m + side]
            parts.append(dot(x, high, NT) + dot(x, low, NT))
        saved_ref[0, m // 2, :, (m % 2) * BLOCK:(m % 2 + 1) * BLOCK] = jnp.where(
            lanes < HALF, parts[0], parts[1]
        )
    for level in range(4):
        outs = []
        for index in range(4):
            state = split(saved_ref[level, index])
            outs.append(dot3(state, (mats_ref[level, index, 0], mats_ref[level, index, 1])))
        if level % 2 == 1:
            outs = regroup(outs)
        for index in range(4):
            if level < 3:
                saved_ref[level + 1, index] = outs[index]
            else:
                rot_scr[:, index * 256:(index + 1) * 256] = outs[index].astype(BF16)
    row = pl.multiple_of(core * ROWS, ROWS)
    column = pl.multiple_of(chip * BLOCK, BLOCK)
    landing = act_ref.at[pl.ds(row, ROWS), pl.ds(column, BLOCK)]
    copies = []
    for k, peer in enumerate(peers):
        source = pl.multiple_of((peer // 2) * BLOCK, BLOCK)
        copy = push(rot_scr.at[:, pl.ds(source, BLOCK)], landing, send.at[k], recv.at[chip], peer)
        copy.start()
        copies.append(copy)
    own = pltpu.make_async_copy(rot_scr.at[:, pl.ds(column, BLOCK)], landing, local)
    own.start()
    own.wait()
    for peer in peers:
        at = pl.multiple_of((peer // 2) * BLOCK, BLOCK)
        arrived(act_ref.at[pl.ds(row, ROWS), pl.ds(at, BLOCK)], recv.at[peer // 2])
    part = act_ref.at[pl.ds(row, ROWS), :]
    copy = push(part, part, fsend, frecv, partner)
    copy.start()
    for other in copies:
        other.wait_send()
    copy.wait_send()
    other_row = pl.multiple_of((1 - core) * ROWS, ROWS)
    arrived(act_ref.at[pl.ds(other_row, ROWS), :], frecv)


def forward(x, cross, local):
    return pl.pallas_call(
        forward_kernel,
        out_shape=(
            jax.ShapeDtypeStruct((4, 4, 2, 256, 256), BF16),
            jax.ShapeDtypeStruct((4, 4, ROWS, 256), F32),
            jax.ShapeDtypeStruct((512, 1024), BF16),
        ),
        in_specs=[VMEM] * 3,
        out_specs=(VMEM, VMEM, ANY),
        scratch_shapes=[
            pltpu.VMEM((ROWS, 1024), BF16), DMA((CHIPS,)), DMA((CHIPS,)), DMA, DMA, DMA,
        ],
        compiler_params=params_of(2),
    )(x, cross, local)


ORDER = [(1, 1), (3, 1), (2, 1), (2, 0), (1, 0), (3, 0), (0, 1), (0, 0)]


def output_kernel(act_ref, cat_ref, out_ref, weights, sends, lands, wsem, send, recv):
    me = lax.axis_index("tensor")
    core = lax.rem(me, 2)
    chip = me // 2
    x_at, y_at = lax.rem(chip, 2), chip // 2
    across = 2 * (chip + 1 - 2 * x_at) + core
    up = 2 * lax.rem(chip + 2, CHIPS) + core
    down = 2 * lax.rem(chip + 6, CHIPS) + core
    fetches = []
    for k, (dy, dx) in enumerate(ORDER):
        target = 2 * lax.rem(y_at + dy, 4) + lax.rem(x_at + dx, 2)
        copy = pltpu.make_async_copy(
            cat_ref.at[:, pl.ds(pl.multiple_of(target * 512, 512), 512)], weights.at[k], wsem.at[k]
        )
        copy.start()
        fetches.append(copy)
    meet([across, up, down])
    started = []

    def product(k, half):
        if half is None:
            return dot(act_ref[...], weights[k])
        return dot(act_ref[half * ROWS:(half + 1) * ROWS], weights[k])

    def give(slot, value, peer):
        sends[slot] = value.astype(BF16)
        copy = push(sends.at[slot], lands.at[slot], send.at[slot], recv.at[slot], peer)
        copy.start()
        started.append(copy)

    def take(slot):
        arrived(lands.at[slot], recv.at[slot])
        return lands[slot].astype(F32)

    fetches[0].wait()
    fetches[1].wait()
    fetches[2].wait()
    for half in range(2):
        give(0 + half, product(0, half), up)
        give(2 + half, product(1, half), down)
        give(4 + half, product(2, half), across)
    fetches[3].wait()
    give(6, product(3, 0) + take(4), up)
    give(7, product(3, 1) + take(5), down)
    fetches[4].wait()
    fetches[5].wait()
    give(8, product(4, 1), up)
    give(9, product(5, 0), down)
    fetches[6].wait()
    for half in range(2):
        give(12 + half, product(6, half) + (take(0 + half) + take(2 + half)), across)
    give(10, product(4, 0) + take(6), up)
    give(11, product(5, 1) + take(7), down)
    fetches[7].wait()
    out_ref[0:ROWS] = product(7, 0) + (take(9) + take(12)) + take(10)
    out_ref[ROWS:] = product(7, 1) + (take(8) + take(13)) + take(11)
    for copy in started:
        copy.wait_send()


def project(act, cat):
    return pl.pallas_call(
        output_kernel,
        out_shape=jax.ShapeDtypeStruct((512, 512), F32),
        in_specs=[VMEM, ANY],
        out_specs=VMEM,
        scratch_shapes=[
            pltpu.VMEM((CHIPS, 1024, 512), BF16),
            pltpu.VMEM((14, ROWS, 512), BF16), pltpu.VMEM((14, ROWS, 512), BF16),
            DMA((CHIPS,)), DMA((14,)), DMA((14,)),
        ],
        compiler_params=params_of(3),
    )(act, cat)


def cotangent_kernel(
    grad_ref, cat_ref, rg_ref, weights, grads, mine, theirs, landed, rounded,
    wsem, gsem, psend, precv, send, recv, local,
):
    me = lax.axis_index("tensor")
    core = lax.rem(me, 2)
    chip = me // 2
    partner = me + 1 - 2 * core
    fetches = []
    for j in range(CHIPS):
        at = pl.multiple_of((2 * j + core) * 512, 512)
        one = pltpu.make_async_copy(cat_ref.at[:, pl.ds(j * 512, 512)], weights.at[j], wsem.at[j])
        two = pltpu.make_async_copy(grad_ref.at[:, pl.ds(at, 512)], grads.at[j], gsem.at[j])
        one.start()
        two.start()
        fetches.append((one, two))
    peers = [lax.rem(me + 2 * k, GROUP) for k in range(1, CHIPS)]
    meet(peers + [partner])
    other_row = pl.multiple_of((1 - core) * ROWS, ROWS)
    row = pl.multiple_of(core * ROWS, ROWS)
    for j in range(CHIPS):
        for copy in fetches[j]:
            copy.wait()
        value = dot(grads[j, pl.ds(other_row, ROWS), :], weights[j], NT)
        if j == 0:
            theirs[...] = value
        else:
            theirs[...] += value
    swap = push(theirs, landed, psend, precv, partner)
    swap.start()
    for j in range(CHIPS):
        value = dot(grads[j, pl.ds(row, ROWS), :], weights[j], NT)
        if j == 0:
            mine[...] = value
        else:
            mine[...] += value
    swap.wait()
    rounded[...] = (mine[...] + landed[...]).astype(BF16)
    column = pl.multiple_of(chip * BLOCK, BLOCK)
    landing = rg_ref.at[:, pl.ds(column, BLOCK)]
    copies = []
    for k, peer in enumerate(peers):
        source = pl.multiple_of((peer // 2) * BLOCK, BLOCK)
        copy = push(rounded.at[:, pl.ds(source, BLOCK)], landing, send.at[k], recv.at[chip], peer)
        copy.start()
        copies.append(copy)
    own = pltpu.make_async_copy(rounded.at[:, pl.ds(column, BLOCK)], landing, local)
    own.start()
    own.wait()
    for peer in peers:
        at = pl.multiple_of((peer // 2) * BLOCK, BLOCK)
        arrived(rg_ref.at[:, pl.ds(at, BLOCK)], recv.at[peer // 2])
    for copy in copies:
        copy.wait_send()


def cotangent(grads, cat):
    return pl.pallas_call(
        cotangent_kernel,
        out_shape=jax.ShapeDtypeStruct((ROWS, 1024), BF16),
        in_specs=[ANY, ANY],
        out_specs=ANY,
        scratch_shapes=[
            pltpu.VMEM((CHIPS, 1024, 512), BF16), pltpu.VMEM((CHIPS, 512, 512), BF16),
            pltpu.VMEM((ROWS, 1024), F32), pltpu.VMEM((ROWS, 1024), F32),
            pltpu.VMEM((ROWS, 1024), F32), pltpu.VMEM((ROWS, 1024), BF16),
            DMA((CHIPS,)), DMA((CHIPS,)), DMA, DMA, DMA((CHIPS,)), DMA((CHIPS,)), DMA,
        ],
        compiler_params=params_of(4),
    )(grads, cat)


def backward_kernel(
    rg_ref, x_ref, saved_ref, mats_ref, own_ref, cross, locals_, cross_in, local_in,
    send, recv, lsend, lrecv, psend, precv,
):
    me = lax.axis_index("tensor")
    core = lax.rem(me, 2)
    chip = me // 2
    partner = me + 1 - 2 * core
    meet([lax.rem(me + k, GROUP) for k in range(1, GROUP)])
    state = [rg_ref[:, index * 256:(index + 1) * 256].astype(F32) for index in range(4)]
    state = regroup(state)
    swaps = []
    for level in (3, 2, 1, 0):
        outs = []
        for index in range(4):
            grad = split(state[index])
            full = dot3(split(saved_ref[level, index]), grad, TN)
            if level % 2 == 0:
                a, b = full[:BLOCK, :BLOCK], full[BLOCK:, BLOCK:]
            else:
                a, b = take_far(full)
            one, two = pairs_of(level, index)
            cross[level, one % 2, one // 2] = a
            cross[level, two % 2, two // 2] = b
            outs.append(dot3(grad, (mats_ref[level, index, 0], mats_ref[level, index, 1]), NT))
        state = regroup(outs) if level == 2 else outs
        copy = push(
            cross.at[level, 1 - core], cross_in.at[level], psend.at[level], precv.at[level], partner
        )
        copy.start()
        swaps.append(copy)
    for m in range(CHIPS):
        grad = split(state[m // 2][:, (m % 2) * BLOCK:(m % 2 + 1) * BLOCK])
        for side in range(2):
            x = x_ref[2 * m + side]
            full = dot(grad[0], x, TN) + dot(grad[1], x, TN)
            locals_[side, m] = full[side * HALF:(side + 1) * HALF]
    copy = push(locals_.at[1 - core], local_in, psend.at[4], precv.at[4], partner)
    copy.start()
    swaps.append(copy)

    def start(src, dst, send_sem, recv_sem, peer):
        @pl.when(peer == me)
        def _():
            pltpu.make_async_copy(src, dst, recv_sem).start()

        @pl.when(peer != me)
        def _():
            push(src, dst, send_sem, recv_sem, peer).start()

    def drain(src, dst, send_sem, recv_sem, peer):
        @pl.when(peer != me)
        def _():
            push(src, dst, send_sem, recv_sem, peer).wait_send()

    jobs = []
    for level in (3, 2, 1, 0):
        swaps[3 - level].wait()
        cross_in[level] = cross_in[level] + cross[level, core]
        for q in range(4):
            peer = pair_owner(2 * q + core, level, chip // 4)
            slot = lax.rem(chip, 4)
            job = (
                cross_in.at[level, q], own_ref.at[4 + 4 * level + slot],
                send.at[level, q], recv.at[level, slot], peer,
            )
            start(*job)
            jobs.append(job)
    swaps[4].wait()
    local_in[...] = local_in[...] + locals_[core]
    for q in range(CHIPS):
        side = pl.multiple_of(lax.rem(chip, 2) * HALF, HALF)
        job = (
            local_in.at[q], own_ref.at[chip // 2, pl.ds(side, HALF), :],
            lsend.at[q], lrecv.at[chip], 2 * q + core,
        )
        start(*job)
        jobs.append(job)
    for job in jobs:
        drain(*job)
    for level in range(4):
        for c in range(4):
            arrived(own_ref.at[4 + 4 * level + c], recv.at[level, c])
    for g in range(CHIPS):
        arrived(own_ref.at[g // 2, pl.ds((g % 2) * HALF, HALF), :], lrecv.at[g])


def backward(rg, x, saved, mats):
    return pl.pallas_call(
        backward_kernel,
        out_shape=jax.ShapeDtypeStruct((20, BLOCK, BLOCK), F32),
        in_specs=[VMEM] * 4,
        out_specs=ANY,
        scratch_shapes=[
            pltpu.VMEM((4, 2, 4, BLOCK, BLOCK), F32), pltpu.VMEM((2, CHIPS, HALF, BLOCK), F32),
            pltpu.VMEM((4, 4, BLOCK, BLOCK), F32), pltpu.VMEM((CHIPS, HALF, BLOCK), F32),
            DMA((4, 4)), DMA((4, 4)), DMA((CHIPS,)), DMA((CHIPS,)), DMA((5,)), DMA((5,)),
        ],
        compiler_params=params_of(5),
    )(rg, x, saved, mats)


def pull_many(inverse, matrix_grad):
    highest = lax.Precision.HIGHEST
    left = jnp.einsum("nji,njk->nik", inverse, matrix_grad, precision=highest)
    full = jnp.einsum("nik,njk->nij", left, inverse, precision=highest)
    return -2.0 * (full - full.transpose(0, 2, 1))


def body(tokens, frozen, local_param, cross_param, out_grad):
    gathered = lax.all_gather(out_grad, "tensor", axis=1, tiled=True)
    x, cat = spread(tokens, frozen)
    cat = cat.reshape(1024, 4096)
    params = jnp.concatenate([local_param, cross_param.reshape(-1, BLOCK, BLOCK)])
    inverse, rotations = inverse_many(params)
    cross, local = route(rotations)
    mats, saved, act = forward(x, cross, local)
    output = project(act, cat)
    rg = cotangent(gathered, cat)
    matrix_grad = backward(rg, x, saved, mats)
    matrix_grad = lax.psum(matrix_grad, "dp")
    matrix_grad = jnp.concatenate([matrix_grad[:4].transpose(0, 2, 1), matrix_grad[4:]])
    grads = pull_many(inverse, matrix_grad)
    return output, grads[:4], grads[4:].reshape(4, 4, BLOCK, BLOCK)


def solution(mesh):
    in_specs = (
        P("dp", "tensor"),
        P("tensor", None),
        P("tensor", None, None),
        P(None, "tensor", None, None),
        P("dp", "tensor"),
    )
    out_specs = (P("dp", "tensor"), P("tensor", None, None), P(None, "tensor", None, None))
    return jax.shard_map(body, mesh=mesh, in_specs=in_specs, out_specs=out_specs, check_vma=False)
```

```python
import functools

import jax
import jax.numpy as jnp
from jax import lax
from jax.experimental import pallas as pl
from jax.experimental.pallas import tpu as pltpu
from jax.sharding import PartitionSpec as P

MESH = pl.DeviceIdType.MESH
F32 = jnp.float32
BF16 = jnp.bfloat16
ANY = pl.BlockSpec(memory_space=pl.ANY)
VMEM = pl.BlockSpec(memory_space=pltpu.VMEM)
DMA = pltpu.SemaphoreType.DMA
GROUP = 16
CHIPS = 8
HALF = 64
BLOCK = 128
ROWS = 256


def params_of(identity, vmem=60):
    return pltpu.CompilerParams(
        collective_id=identity, has_side_effects=True, vmem_limit_bytes=vmem << 20
    )


def meet(peers, axis="tensor"):
    barrier = pltpu.get_barrier_semaphore()
    for peer in peers:
        pl.semaphore_signal(barrier, inc=1, device_id={axis: peer}, device_id_type=MESH)
    pl.semaphore_wait(barrier, len(peers))


def push(src, dst, send, recv, peer, axis="tensor"):
    return pltpu.make_async_remote_copy(
        src_ref=src, dst_ref=dst, send_sem=send, recv_sem=recv,
        device_id={axis: peer}, device_id_type=MESH,
    )


def start_job(src, dst, send, recv, peer, me):
    @pl.when(peer == me)
    def _():
        pltpu.make_async_copy(src, dst, recv).start()

    @pl.when(peer != me)
    def _():
        push(src, dst, send, recv, peer).start()


def drain_job(src, dst, send, recv, peer, me):
    @pl.when(peer != me)
    def _():
        push(src, dst, send, recv, peer).wait_send()


def arrived(ref, sem):
    pltpu.make_async_copy(ref, ref, sem).wait()


def split(value):
    high = value.astype(BF16)
    return high, (value - high.astype(F32)).astype(BF16)


def dot(a, b, dims=(((1,), (0,)), ((), ()))):
    return lax.dot_general(a, b, dims, preferred_element_type=F32)


NT = (((1,), (1,)), ((), ()))
TN = (((0,), (0,)), ((), ()))


def dot3(a, b, dims=(((1,), (0,)), ((), ()))):
    return dot(a[0], b[0], dims) + (dot(a[0], b[1], dims) + dot(a[1], b[0], dims))


def inverse_blocks(param_ref, out_ref, rot_ref):
    count, size, _ = param_ref.shape
    step = 32
    rows = lax.broadcasted_iota(jnp.int32, (size, size), 0)
    lanes = lax.broadcasted_iota(jnp.int32, (size, size), 1)
    panel_rows = lax.broadcasted_iota(jnp.int32, (step, size), 0)
    panel_lanes = lax.broadcasted_iota(jnp.int32, (step, size), 1)
    identity = jnp.where(rows == lanes, 1.0, 0.0)
    for at in range(count):
        param = param_ref[at]
        out_ref[at] = identity + param - param.T

    def eliminate(block_at, carry):
        start = pl.multiple_of(block_at * step, step)
        shift = lax.rem(size - start, size)
        inside = (lanes >= start) & (lanes < start + step)
        panels = [pltpu.roll(out_ref[at, pl.ds(start, step), :], shift, 1) for at in range(count)]
        for k in range(step):
            for at in range(count):
                panel = panels[at]
                column = panel[:, k:k + 1]
                scale = 1.0 / panel[k:k + 1, k:k + 1]
                row = jnp.where(panel_lanes[:1] == k, 1.0, panel[k:k + 1, :]) * scale
                rest = jnp.where(panel_lanes == k, 0.0, panel) - column * row
                panels[at] = jnp.where(panel_rows == k, row, rest)
        panels = [pltpu.roll(panel, start, 1) for panel in panels]
        for at in range(count):
            matrix = out_ref[at]
            turned = pltpu.roll(matrix, shift, 1)[:, :step]
            out_ref[at] = jnp.where(inside, 0.0, matrix) - jnp.dot(
                turned, panels[at], precision=lax.Precision.HIGHEST, preferred_element_type=F32
            )
        for at in range(count):
            out_ref[at, pl.ds(start, step), :] = panels[at]
        return carry

    lax.fori_loop(0, size // step, eliminate, 0)
    for at in range(count):
        rotation = 2.0 * out_ref[at] - identity
        rot_ref[at] = rotation.T if at < 4 else rotation


def pair_place(me, level):
    low = 2 ** level
    bit = lax.rem(me // low, 2)
    pair = (me // (2 * low)) * low + lax.rem(me, low)
    return bit, pair


def pair_owner(pair, level, bit):
    low = 2 ** level
    return (pair // low) * (2 * low) + bit * low + lax.rem(pair, low)


def mix(a, b, r):
    at = (r // 2) * BLOCK
    first, second = a[:, at:at + BLOCK], b[:, at:at + BLOCK]
    lanes = lax.broadcasted_iota(jnp.int32, first.shape, 1)
    if r % 2 == 0:
        return jnp.where(lanes < HALF, first, pltpu.roll(second, HALF, 1))
    return jnp.where(lanes < HALF, pltpu.roll(first, HALF, 1), second)


def regroup(quads):
    return [
        jnp.concatenate([mix(quads[0], quads[1], r), mix(quads[2], quads[3], r)], axis=1)
        for r in range(4)
    ]


def place_near(a, b):
    zero = jnp.zeros((BLOCK, BLOCK), F32)
    return jnp.concatenate(
        [jnp.concatenate([a, zero], axis=1), jnp.concatenate([zero, b], axis=1)], axis=0
    )


def place_far(a, b):
    lanes = lax.broadcasted_iota(jnp.int32, (BLOCK, BLOCK), 1)
    turned_a, turned_b = pltpu.roll(a, HALF, 1), pltpu.roll(b, HALF, 1)
    low = lanes < HALF
    a_rows = jnp.concatenate([jnp.where(low, a, 0.0), jnp.where(low, turned_a, 0.0)], axis=1)
    b_rows = jnp.concatenate([jnp.where(low, 0.0, turned_b), jnp.where(low, 0.0, b)], axis=1)
    return jnp.concatenate(
        [a_rows[:HALF], b_rows[:HALF], a_rows[HALF:], b_rows[HALF:]], axis=0
    )


def take_far(full):
    lanes = lax.broadcasted_iota(jnp.int32, (BLOCK, BLOCK), 1)
    low = lanes < HALF
    a_rows = jnp.concatenate([full[:HALF], full[BLOCK:BLOCK + HALF]], axis=0)
    b_rows = jnp.concatenate([full[HALF:BLOCK], full[BLOCK + HALF:]], axis=0)
    a = jnp.where(low, a_rows[:, :BLOCK], pltpu.roll(a_rows[:, BLOCK:], HALF, 1))
    b = jnp.where(low, pltpu.roll(b_rows[:, :BLOCK], HALF, 1), b_rows[:, BLOCK:])
    return a, b


def pairs_of(level, index):
    if level < 2:
        return 2 * index, 2 * index + 1
    return index, 4 + index


def start_kernel(
    tok_ref, froz_ref, param_ref,
    x_ref, cat_ref, inv_ref, mats_ref, saved_ref, act_ref,
    x_scr, rot, cross, local, mats, saved, rotated,
    tsend, trecv, fsend, frecv, send, recv, lsend, lrecv, psend, precv, asend, arecv, wsem,
):
    me = lax.axis_index("tensor")
    core = lax.rem(me, 2)
    chip = me // 2
    partner = me + 1 - 2 * core
    others = [lax.rem(me + k, GROUP) for k in range(1, GROUP)]
    meet(others)

    def token_slice(peer):
        column = pl.multiple_of((peer // 4) * BLOCK, BLOCK)
        row = pl.multiple_of(lax.rem(peer, 2) * ROWS, ROWS)
        return tok_ref.at[pl.ds(row, ROWS), pl.ds(column, BLOCK)]

    sends = []
    for k, peer in enumerate(others):
        copy = push(token_slice(peer), x_scr.at[me], tsend.at[k], trecv.at[me], peer)
        copy.start()
        sends.append(copy)
    pltpu.make_async_copy(token_slice(me), x_scr.at[me], trecv.at[me]).start()
    for j in range(CHIPS):
        theirs = pl.multiple_of((2 * j + 1 - core) * 512, 512)
        target = cat_ref.at[:, :, pl.ds(j * 512, 512)]
        copy = push(froz_ref.at[:, :, pl.ds(theirs, 512)], target, fsend.at[j], frecv.at[j], partner)
        copy.start()
        sends.append(copy)

    inverse_blocks(param_ref, inv_ref, rot)

    jobs = []
    for k in range(4):
        c = lax.rem(chip + k, 4)
        for side in range(2):
            jobs.append((
                rot.at[c, pl.ds(side * HALF, HALF), :], local.at[chip, core],
                lsend.at[k, side], lrecv.at[chip], 2 * (2 * c + side) + core, me,
            ))
    for level in range(4):
        bit, pair = pair_place(me, level)
        for k in range(4):
            c = lax.rem(chip + k, 4)
            jobs.append((
                rot.at[4 + 4 * level + c], cross.at[level, pair // 2, lax.rem(pair, 2)],
                send.at[level, k], recv.at[level, pair // 2],
                2 * (c + 4 * bit) + lax.rem(pair, 2), me,
            ))
    for job in jobs:
        start_job(*job)
    writes = []

    def forward_on(stage):
        if stage == 0:
            for q in range(CHIPS):
                arrived(local.at[q, core], lrecv.at[q])
            part = local.at[:, core]
        else:
            for q in range(4):
                arrived(cross.at[stage - 1, q, core], recv.at[stage - 1, q])
            part = cross.at[stage - 1, :, core]
        copy = push(part, part, psend.at[stage], precv.at[stage], partner)
        copy.start()
        sends.append(copy)

    forward_on(0)
    forward_on(1)
    for peer in [me] + others:
        arrived(x_scr.at[peer], trecv.at[peer])
    copy = pltpu.make_async_copy(x_scr, x_ref, wsem.at[0])
    copy.start()
    writes.append(copy)
    arrived(local.at[:, 1 - core], precv.at[0])
    lanes = lax.broadcasted_iota(jnp.int32, (ROWS, BLOCK), 1)
    for m in range(CHIPS):
        parts = []
        for side in range(2):
            high, low = split(jnp.concatenate([local[m, side]] * 2, axis=0))
            x = x_scr[2 * m + side]
            parts.append(dot(x, high, NT) + dot(x, low, NT))
        saved[0, m // 2, :, (m % 2) * BLOCK:(m % 2 + 1) * BLOCK] = jnp.where(
            lanes < HALF, parts[0], parts[1]
        )
    for level in range(4):
        if level < 3:
            forward_on(level + 2)
        copy = pltpu.make_async_copy(saved.at[level], saved_ref.at[level], wsem.at[1 + level])
        copy.start()
        writes.append(copy)
        arrived(cross.at[level, :, 1 - core], precv.at[level + 1])
        outs = []
        for index in range(4):
            one, two = pairs_of(level, index)
            a = cross[level, one // 2, one % 2]
            b = cross[level, two // 2, two % 2]
            matrix = split(place_near(a, b) if level % 2 == 0 else place_far(a, b))
            mats[level, index, 0] = matrix[0]
            mats[level, index, 1] = matrix[1]
            outs.append(dot3(split(saved[level, index]), matrix))
        copy = pltpu.make_async_copy(mats.at[level], mats_ref.at[level], wsem.at[5 + level])
        copy.start()
        writes.append(copy)
        if level % 2 == 1:
            outs = regroup(outs)
        for index in range(4):
            if level < 3:
                saved[level + 1, index] = outs[index]
            else:
                rotated[:, index * 256:(index + 1) * 256] = outs[index].astype(BF16)
    row = pl.multiple_of(core * ROWS, ROWS)
    column = pl.multiple_of(chip * BLOCK, BLOCK)
    landing = act_ref.at[pl.ds(row, ROWS), pl.ds(column, BLOCK)]
    peers = [lax.rem(me + 2 * k, GROUP) for k in range(1, CHIPS)]
    for k, peer in enumerate(peers):
        source = pl.multiple_of((peer // 2) * BLOCK, BLOCK)
        copy = push(rotated.at[:, pl.ds(source, BLOCK)], landing, asend.at[k], arecv.at[chip], peer)
        copy.start()
        sends.append(copy)
    pltpu.make_async_copy(rotated.at[:, pl.ds(column, BLOCK)], landing, arecv.at[chip]).start()
    for peer in [me] + peers:
        at = pl.multiple_of((peer // 2) * BLOCK, BLOCK)
        arrived(act_ref.at[pl.ds(row, ROWS), pl.ds(at, BLOCK)], arecv.at[peer // 2])
    part = act_ref.at[pl.ds(row, ROWS), :]
    copy = push(part, part, psend.at[5], precv.at[5], partner)
    copy.start()
    sends.append(copy)
    for copy in writes:
        copy.wait()
    for copy in sends:
        copy.wait_send()
    for job in jobs:
        drain_job(*job)
    for j in range(CHIPS):
        arrived(cat_ref.at[:, :, pl.ds(j * 512, 512)], frecv.at[j])
    other_row = pl.multiple_of((1 - core) * ROWS, ROWS)
    arrived(act_ref.at[pl.ds(other_row, ROWS), :], precv.at[5])


def start(tokens, frozen, params):
    return pl.pallas_call(
        start_kernel,
        out_shape=(
            jax.ShapeDtypeStruct((GROUP, ROWS, BLOCK), BF16),
            jax.ShapeDtypeStruct((CHIPS, HALF, 4096), BF16),
            jax.ShapeDtypeStruct((20, BLOCK, BLOCK), F32),
            jax.ShapeDtypeStruct((4, 4, 2, 256, 256), BF16),
            jax.ShapeDtypeStruct((4, 4, ROWS, 256), F32),
            jax.ShapeDtypeStruct((512, 1024), BF16),
        ),
        in_specs=[ANY, ANY, VMEM],
        out_specs=(ANY, ANY, VMEM, ANY, ANY, ANY),
        scratch_shapes=[
            pltpu.VMEM((GROUP, ROWS, BLOCK), BF16), pltpu.VMEM((20, BLOCK, BLOCK), F32),
            pltpu.VMEM((4, 4, 2, BLOCK, BLOCK), F32), pltpu.VMEM((CHIPS, 2, HALF, BLOCK), F32),
            pltpu.VMEM((4, 4, 2, 256, 256), BF16), pltpu.VMEM((4, 4, ROWS, 256), F32),
            pltpu.VMEM((ROWS, 1024), BF16),
            DMA((GROUP,)), DMA((GROUP,)), DMA((CHIPS,)), DMA((CHIPS,)),
            DMA((4, 4)), DMA((4, 4)), DMA((4, 2)), DMA((CHIPS,)), DMA((6,)), DMA((6,)),
            DMA((CHIPS,)), DMA((CHIPS,)), DMA((9,)),
        ],
        compiler_params=params_of(0),
    )(tokens, frozen.reshape(CHIPS, HALF, 8192), params)


ORDER = [(1, 1), (3, 1), (2, 1), (2, 0), (1, 0), (3, 0), (0, 1), (0, 0)]


def finish_kernel(
    act_hbm, froz_ref, cat_ref, grad_ref, x_hbm, saved_hbm, mats_hbm,
    out_ref, own_ref,
    act, weights, grads, x_ref, saved, mats, sends, lands, mine, theirs, landed, rounded, rg,
    cross, locals_, cross_in, local_in,
    wsem, gsem, hsem, send, recv, psend, precv, rsend, rrecv, msend, mrecv, lsend, lrecv,
):
    me = lax.axis_index("tensor")
    core = lax.rem(me, 2)
    chip = me // 2
    partner = me + 1 - 2 * core
    x_at, y_at = lax.rem(chip, 2), chip // 2
    across = 2 * (chip + 1 - 2 * x_at) + core
    up = 2 * lax.rem(chip + 2, CHIPS) + core
    down = 2 * lax.rem(chip + 6, CHIPS) + core
    load = pltpu.make_async_copy(act_hbm, act, hsem.at[0])
    load.start()
    fetches = []
    for k, (dy, dx) in enumerate(ORDER):
        target = 2 * lax.rem(y_at + dy, 4) + lax.rem(x_at + dx, 2)
        at = pl.multiple_of((2 * target + core) * 512, 512)
        one = pltpu.make_async_copy(
            froz_ref.at[:, :, pl.ds(at, 512)], weights.at[k, :, core], wsem.at[k, 0]
        )
        two = pltpu.make_async_copy(
            cat_ref.at[:, :, pl.ds(pl.multiple_of(target * 512, 512), 512)],
            weights.at[k, :, 1 - core], wsem.at[k, 1],
        )
        one.start()
        two.start()
        fetches.append((one, two))
    gets = []
    for k, (dy, dx) in enumerate(ORDER):
        target = 2 * lax.rem(y_at + dy, 4) + lax.rem(x_at + dx, 2)
        at = pl.multiple_of((2 * target + core) * 512, 512)
        copy = pltpu.make_async_copy(grad_ref.at[:, pl.ds(at, 512)], grads.at[k], gsem.at[k])
        copy.start()
        gets.append(copy)
    later = []
    for level in (3, 2, 1, 0):
        one = pltpu.make_async_copy(saved_hbm.at[level], saved.at[level], hsem.at[1 + level])
        two = pltpu.make_async_copy(mats_hbm.at[level], mats.at[level], hsem.at[5 + level])
        one.start()
        two.start()
        later.append((one, two))
    x_get = pltpu.make_async_copy(x_hbm, x_ref, hsem.at[9])
    x_get.start()
    meet([lax.rem(me + k, GROUP) for k in range(1, GROUP)])
    started = []

    def product(k, half):
        return dot(act[half * ROWS:(half + 1) * ROWS], weights[k].reshape(1024, 512))

    def fetched(k):
        for copy in fetches[k]:
            copy.wait()

    def give(slot, value, peer):
        sends[slot] = value.astype(BF16)
        copy = push(sends.at[slot], lands.at[slot], send.at[slot], recv.at[slot], peer)
        copy.start()
        started.append(copy)

    def take(slot):
        arrived(lands.at[slot], recv.at[slot])
        return lands[slot].astype(F32)

    load.wait()
    for half in range(2):
        for k, peer in ((0, up), (1, down), (2, across)):
            if half == 0:
                fetched(k)
            give(2 * k + half, product(k, half), peer)
    fetched(3)
    fetched(4)
    fetched(5)
    give(8, product(4, 1), up)
    give(9, product(5, 0), down)
    fetched(6)
    fetched(7)
    for copy in gets:
        copy.wait()
    other_row = pl.multiple_of((1 - core) * ROWS, ROWS)
    row = pl.multiple_of(core * ROWS, ROWS)
    for k in range(CHIPS):
        value = dot(grads[k, pl.ds(other_row, ROWS), :], weights[k].reshape(1024, 512), NT)
        if k == 0:
            theirs[...] = value
        else:
            theirs[...] += value
    swap = push(theirs, landed, psend.at[5], precv.at[5], partner)
    swap.start()
    give(6, product(3, 0) + take(4), up)
    give(7, product(3, 1) + take(5), down)
    for k in range(CHIPS):
        value = dot(grads[k, pl.ds(row, ROWS), :], weights[k].reshape(1024, 512), NT)
        if k == 0:
            mine[...] = value
        else:
            mine[...] += value
    swap.wait()
    rounded[...] = (mine[...] + landed[...]).astype(BF16)
    column = pl.multiple_of(chip * BLOCK, BLOCK)
    landing = rg.at[:, pl.ds(column, BLOCK)]
    peers = [lax.rem(me + 2 * k, GROUP) for k in range(1, CHIPS)]
    for k, peer in enumerate(peers):
        source = pl.multiple_of((peer // 2) * BLOCK, BLOCK)
        copy = push(rounded.at[:, pl.ds(source, BLOCK)], landing, rsend.at[k], rrecv.at[chip], peer)
        copy.start()
        started.append(copy)
    pltpu.make_async_copy(rounded.at[:, pl.ds(column, BLOCK)], landing, rrecv.at[chip]).start()
    for half in range(2):
        give(12 + half, product(6, half) + (take(0 + half) + take(2 + half)), across)
    give(10, product(4, 0) + take(6), up)
    give(11, product(5, 1) + take(7), down)
    for peer in [me] + peers:
        at = pl.multiple_of((peer // 2) * BLOCK, BLOCK)
        arrived(rg.at[:, pl.ds(at, BLOCK)], rrecv.at[peer // 2])

    state = [rg[:, index * 256:(index + 1) * 256].astype(F32) for index in range(4)]
    state = regroup(state)
    swaps = []
    for level in (3, 2, 1, 0):
        for copy in later[3 - level]:
            copy.wait()
        outs = []
        for index in range(4):
            grad = split(state[index])
            full = dot3(split(saved[level, index]), grad, TN)
            if level % 2 == 0:
                a, b = full[:BLOCK, :BLOCK], full[BLOCK:, BLOCK:]
            else:
                a, b = take_far(full)
            one, two = pairs_of(level, index)
            cross[level, one % 2, one // 2] = a
            cross[level, two % 2, two // 2] = b
            outs.append(dot3(grad, (mats[level, index, 0], mats[level, index, 1]), NT))
        state = regroup(outs) if level == 2 else outs
        copy = push(
            cross.at[level, 1 - core], cross_in.at[level], psend.at[level], precv.at[level], partner
        )
        copy.start()
        swaps.append(copy)
    x_get.wait()
    for m in range(CHIPS):
        grad = split(state[m // 2][:, (m % 2) * BLOCK:(m % 2 + 1) * BLOCK])
        for side in range(2):
            x = x_ref[2 * m + side]
            full = dot(grad[0], x, TN) + dot(grad[1], x, TN)
            locals_[side, m] = full[side * HALF:(side + 1) * HALF]
    copy = push(locals_.at[1 - core], local_in, psend.at[4], precv.at[4], partner)
    copy.start()
    swaps.append(copy)

    jobs = []
    for level in (3, 2, 1, 0):
        swaps[3 - level].wait()
        cross_in[level] = cross_in[level] + cross[level, core]
        slot = lax.rem(chip, 4)
        for k in range(4):
            q = lax.rem(chip + k, 4)
            job = (
                cross_in.at[level, q], own_ref.at[4 + 4 * level + slot],
                msend.at[level, k], mrecv.at[level, slot],
                pair_owner(2 * q + core, level, chip // 4), me,
            )
            start_job(*job)
            jobs.append(job)
    swaps[4].wait()
    local_in[...] = local_in[...] + locals_[core]
    for k in range(CHIPS):
        q = lax.rem(chip + k, CHIPS)
        side = pl.multiple_of(lax.rem(chip, 2) * HALF, HALF)
        job = (
            local_in.at[q], own_ref.at[chip // 2, pl.ds(side, HALF), :],
            lsend.at[k], lrecv.at[chip], 2 * q + core, me,
        )
        start_job(*job)
        jobs.append(job)
    out_ref[0:ROWS] = product(7, 0) + (take(9) + take(12)) + take(10)
    out_ref[ROWS:] = product(7, 1) + (take(8) + take(13)) + take(11)
    for copy in started:
        copy.wait_send()
    for job in jobs:
        drain_job(*job)
    for level in range(4):
        for c in range(4):
            arrived(own_ref.at[4 + 4 * level + c], mrecv.at[level, c])
    for g in range(CHIPS):
        arrived(own_ref.at[g // 2, pl.ds((g % 2) * HALF, HALF), :], lrecv.at[g])


def finish(act, frozen, cat, grads, x, saved, mats):
    return pl.pallas_call(
        finish_kernel,
        out_shape=(
            jax.ShapeDtypeStruct((512, 512), F32), jax.ShapeDtypeStruct((20, BLOCK, BLOCK), F32),
        ),
        in_specs=[ANY] * 7,
        out_specs=(VMEM, ANY),
        scratch_shapes=[
            pltpu.VMEM((512, 1024), BF16), pltpu.VMEM((CHIPS, CHIPS, 2, HALF, 512), BF16),
            pltpu.VMEM((CHIPS, 512, 512), BF16), pltpu.VMEM((GROUP, ROWS, BLOCK), BF16),
            pltpu.VMEM((4, 4, ROWS, 256), F32), pltpu.VMEM((4, 4, 2, 256, 256), BF16),
            pltpu.VMEM((14, ROWS, 512), BF16), pltpu.VMEM((14, ROWS, 512), BF16),
            pltpu.VMEM((ROWS, 1024), F32), pltpu.VMEM((ROWS, 1024), F32),
            pltpu.VMEM((ROWS, 1024), F32), pltpu.VMEM((ROWS, 1024), BF16),
            pltpu.VMEM((ROWS, 1024), BF16),
            pltpu.VMEM((4, 2, 4, BLOCK, BLOCK), F32), pltpu.VMEM((2, CHIPS, HALF, BLOCK), F32),
            pltpu.VMEM((4, 4, BLOCK, BLOCK), F32), pltpu.VMEM((CHIPS, HALF, BLOCK), F32),
            DMA((CHIPS, 2)), DMA((CHIPS,)), DMA((10,)), DMA((14,)), DMA((14,)), DMA((6,)), DMA((6,)),
            DMA((CHIPS,)), DMA((CHIPS,)), DMA((4, 4)), DMA((4, 4)), DMA((CHIPS,)), DMA((CHIPS,)),
        ],
        compiler_params=params_of(1),
    )(act, frozen.reshape(CHIPS, HALF, 8192), cat, grads, x, saved, mats)


def total_kernel(own_ref, out_ref, landed, part, send, recv, gsend, grecv):
    me = lax.axis_index("dp")
    others = [lax.rem(me + k, 8) for k in range(1, 8)]
    meet(others, "dp")
    copies = []
    for k, peer in enumerate(others):
        rows = own_ref.at[:, pl.ds(pl.multiple_of(peer * 16, 16), 16), :]
        copy = push(rows, landed.at[me], send.at[k], recv.at[me], peer, "dp")
        copy.start()
        copies.append(copy)
    mine = pl.ds(pl.multiple_of(me * 16, 16), 16)
    value = own_ref[:, mine, :]
    for peer in others:
        arrived(landed.at[peer], recv.at[peer])
        value = value + landed[peer]
    part[...] = value
    out_ref[:, mine, :] = value
    for k, peer in enumerate(others):
        copy = push(part, out_ref.at[:, mine, :], gsend.at[k], grecv.at[me], peer, "dp")
        copy.start()
        copies.append(copy)
    for peer in others:
        rows = out_ref.at[:, pl.ds(pl.multiple_of(peer * 16, 16), 16), :]
        arrived(rows, grecv.at[peer])
    for copy in copies:
        copy.wait_send()


def total(own):
    return pl.pallas_call(
        total_kernel,
        out_shape=jax.ShapeDtypeStruct((20, BLOCK, BLOCK), F32),
        in_specs=[VMEM],
        out_specs=VMEM,
        scratch_shapes=[
            pltpu.VMEM((8, 20, 16, BLOCK), F32), pltpu.VMEM((20, 16, BLOCK), F32),
            DMA((8,)), DMA((8,)), DMA((8,)), DMA((8,)),
        ],
        compiler_params=params_of(2),
    )(own)


def pull_many(inverse, matrix_grad):
    highest = lax.Precision.HIGHEST
    left = jnp.einsum("nji,njk->nik", inverse, matrix_grad, precision=highest)
    full = jnp.einsum("nik,njk->nij", left, inverse, precision=highest)
    return -2.0 * (full - full.transpose(0, 2, 1))


def body(tokens, frozen, local_param, cross_param, out_grad):
    gathered = lax.all_gather(out_grad, "tensor", axis=1, tiled=True)
    params = jnp.concatenate([local_param, cross_param.reshape(-1, BLOCK, BLOCK)])
    x, cat, inverse, mats, saved, act = start(tokens, frozen, params)
    output, own = finish(act, frozen, cat, gathered, x, saved, mats)
    matrix_grad = total(own)
    matrix_grad = jnp.concatenate([matrix_grad[:4].transpose(0, 2, 1), matrix_grad[4:]])
    grads = pull_many(inverse, matrix_grad)
    return output, grads[:4], grads[4:].reshape(4, 4, BLOCK, BLOCK)


def solution(mesh):
    in_specs = (
        P("dp", "tensor"),
        P("tensor", None),
        P("tensor", None, None),
        P(None, "tensor", None, None),
        P("dp", "tensor"),
    )
    out_specs = (P("dp", "tensor"), P("tensor", None, None), P(None, "tensor", None, None))
    return jax.shard_map(body, mesh=mesh, in_specs=in_specs, out_specs=out_specs, check_vma=False)
```

```python
import functools

import jax
import jax.numpy as jnp
from jax import lax
from jax.experimental import pallas as pl
from jax.experimental.pallas import tpu as pltpu
from jax.sharding import PartitionSpec as P

MESH = pl.DeviceIdType.MESH
F32 = jnp.float32
BF16 = jnp.bfloat16
ANY = pl.BlockSpec(memory_space=pl.ANY)
VMEM = pl.BlockSpec(memory_space=pltpu.VMEM)
DMA = pltpu.SemaphoreType.DMA
GROUP = 16
CHIPS = 8
HALF = 64
BLOCK = 128
ROWS = 256


def params_of(identity, vmem=60):
    return pltpu.CompilerParams(
        collective_id=identity, has_side_effects=True, vmem_limit_bytes=vmem << 20
    )


def meet(peers, axis="tensor"):
    barrier = pltpu.get_barrier_semaphore()
    for peer in peers:
        pl.semaphore_signal(barrier, inc=1, device_id={axis: peer}, device_id_type=MESH)
    pl.semaphore_wait(barrier, len(peers))


def push(src, dst, send, recv, peer, axis="tensor"):
    return pltpu.make_async_remote_copy(
        src_ref=src, dst_ref=dst, send_sem=send, recv_sem=recv,
        device_id={axis: peer}, device_id_type=MESH,
    )


def start_job(src, dst, send, recv, peer, me):
    @pl.when(peer == me)
    def _():
        pltpu.make_async_copy(src, dst, recv).start()

    @pl.when(peer != me)
    def _():
        push(src, dst, send, recv, peer).start()


def drain_job(src, dst, send, recv, peer, me):
    @pl.when(peer != me)
    def _():
        push(src, dst, send, recv, peer).wait_send()


def arrived(ref, sem):
    pltpu.make_async_copy(ref, ref, sem).wait()


def split(value):
    high = value.astype(BF16)
    return high, (value - high.astype(F32)).astype(BF16)


def dot(a, b, dims=(((1,), (0,)), ((), ()))):
    return lax.dot_general(a, b, dims, preferred_element_type=F32)


NT = (((1,), (1,)), ((), ()))
TN = (((0,), (0,)), ((), ()))


def dot3(a, b, dims=(((1,), (0,)), ((), ()))):
    return dot(a[0], b[0], dims) + (dot(a[0], b[1], dims) + dot(a[1], b[0], dims))


def inverse_blocks(local_param, cross_param, out_ref, rot_ref):
    count, size, _ = out_ref.shape
    step = 32
    rows = lax.broadcasted_iota(jnp.int32, (size, size), 0)
    lanes = lax.broadcasted_iota(jnp.int32, (size, size), 1)
    panel_rows = lax.broadcasted_iota(jnp.int32, (step, size), 0)
    panel_lanes = lax.broadcasted_iota(jnp.int32, (step, size), 1)
    identity = jnp.where(rows == lanes, 1.0, 0.0)
    for at in range(count):
        param = local_param[at] if at < 4 else cross_param[(at - 4) // 4, at % 4]
        out_ref[at] = identity + param - param.T

    def eliminate(block_at, carry):
        start = pl.multiple_of(block_at * step, step)
        shift = lax.rem(size - start, size)
        inside = (lanes >= start) & (lanes < start + step)
        panels = [pltpu.roll(out_ref[at, pl.ds(start, step), :], shift, 1) for at in range(count)]
        for k in range(step):
            for at in range(count):
                panel = panels[at]
                column = panel[:, k:k + 1]
                scale = 1.0 / panel[k:k + 1, k:k + 1]
                row = jnp.where(panel_lanes[:1] == k, 1.0, panel[k:k + 1, :]) * scale
                rest = jnp.where(panel_lanes == k, 0.0, panel) - column * row
                panels[at] = jnp.where(panel_rows == k, row, rest)
        panels = [pltpu.roll(panel, start, 1) for panel in panels]
        for at in range(count):
            matrix = out_ref[at]
            turned = pltpu.roll(matrix, shift, 1)[:, :step]
            out_ref[at] = jnp.where(inside, 0.0, matrix) - jnp.dot(
                turned, panels[at], precision=lax.Precision.HIGHEST, preferred_element_type=F32
            )
        for at in range(count):
            out_ref[at, pl.ds(start, step), :] = panels[at]
        return carry

    lax.fori_loop(0, size // step, eliminate, 0)
    for at in range(count):
        rotation = 2.0 * out_ref[at] - identity
        rot_ref[at] = rotation.T if at < 4 else rotation


def pair_place(me, level):
    low = 2 ** level
    bit = lax.rem(me // low, 2)
    pair = (me // (2 * low)) * low + lax.rem(me, low)
    return bit, pair


def pair_owner(pair, level, bit):
    low = 2 ** level
    return (pair // low) * (2 * low) + bit * low + lax.rem(pair, low)


def mix(a, b, r):
    at = (r // 2) * BLOCK
    first, second = a[:, at:at + BLOCK], b[:, at:at + BLOCK]
    lanes = lax.broadcasted_iota(jnp.int32, first.shape, 1)
    if r % 2 == 0:
        return jnp.where(lanes < HALF, first, pltpu.roll(second, HALF, 1))
    return jnp.where(lanes < HALF, pltpu.roll(first, HALF, 1), second)


def regroup(quads):
    return [
        jnp.concatenate([mix(quads[0], quads[1], r), mix(quads[2], quads[3], r)], axis=1)
        for r in range(4)
    ]


def place_near(a, b):
    zero = jnp.zeros((BLOCK, BLOCK), F32)
    return jnp.concatenate(
        [jnp.concatenate([a, zero], axis=1), jnp.concatenate([zero, b], axis=1)], axis=0
    )


def place_far(a, b):
    lanes = lax.broadcasted_iota(jnp.int32, (BLOCK, BLOCK), 1)
    turned_a, turned_b = pltpu.roll(a, HALF, 1), pltpu.roll(b, HALF, 1)
    low = lanes < HALF
    a_rows = jnp.concatenate([jnp.where(low, a, 0.0), jnp.where(low, turned_a, 0.0)], axis=1)
    b_rows = jnp.concatenate([jnp.where(low, 0.0, turned_b), jnp.where(low, 0.0, b)], axis=1)
    return jnp.concatenate(
        [a_rows[:HALF], b_rows[:HALF], a_rows[HALF:], b_rows[HALF:]], axis=0
    )


def take_far(full):
    lanes = lax.broadcasted_iota(jnp.int32, (BLOCK, BLOCK), 1)
    low = lanes < HALF
    a_rows = jnp.concatenate([full[:HALF], full[BLOCK:BLOCK + HALF]], axis=0)
    b_rows = jnp.concatenate([full[HALF:BLOCK], full[BLOCK + HALF:]], axis=0)
    a = jnp.where(low, a_rows[:, :BLOCK], pltpu.roll(a_rows[:, BLOCK:], HALF, 1))
    b = jnp.where(low, pltpu.roll(b_rows[:, :BLOCK], HALF, 1), b_rows[:, BLOCK:])
    return a, b


def pairs_of(level, index):
    if level < 2:
        return 2 * index, 2 * index + 1
    return index, 4 + index


ORDER = [(1, 1), (3, 1), (2, 1), (2, 0), (1, 0), (3, 0), (0, 1), (0, 0)]


def layer_kernel(
    tok_ref, froz_ref, grad_ref, local_param, cross_param,
    out_ref, own_ref, inv_ref,
    x_scr, rot, cross, local, mats, saved, rotated, act, weights, grads, sends_buf, lands,
    mine, theirs, landed, rounded, rg, grad_cross, grad_local, cross_in, local_in,
    tsend, trecv, fsend, frecv, wsem, send, recv, lsend, lrecv, psend, precv, asend, arecv,
    gsend, grecv, osend, orecv, rsend, rrecv, bsend, brecv, msend, mrecv, nsend, nrecv,
):
    me = lax.axis_index("tensor")
    core = lax.rem(me, 2)
    chip = me // 2
    partner = me + 1 - 2 * core
    x_at, y_at = lax.rem(chip, 2), chip // 2
    across = 2 * (chip + 1 - 2 * x_at) + core
    up = 2 * lax.rem(chip + 2, CHIPS) + core
    down = 2 * lax.rem(chip + 6, CHIPS) + core
    others = [lax.rem(me + k, GROUP) for k in range(1, GROUP)]
    peers = [lax.rem(me + 2 * k, GROUP) for k in range(1, CHIPS)]
    row = pl.multiple_of(core * ROWS, ROWS)
    other_row = pl.multiple_of((1 - core) * ROWS, ROWS)
    column = pl.multiple_of(chip * BLOCK, BLOCK)
    sends = []

    def go(copy):
        copy.start()
        sends.append(copy)

    def place(dy, dx):
        return ORDER.index((dy, dx))

    def gather(src, slot, half, peer):
        part = src if half is None else src.at[pl.ds(half * ROWS, ROWS), :]
        dst = grads.at[slot] if half is None else grads.at[slot, pl.ds(half * ROWS, ROWS), :]
        at = len(ORDER) if half == 1 else slot
        go(push(part, dst, gsend.at[at], grecv.at[at], peer))

    def gathered(slot, half=None):
        dst = grads.at[slot] if half is None else grads.at[slot, pl.ds(half * ROWS, ROWS), :]
        arrived(dst, grecv.at[len(ORDER) if half == 1 else slot])

    pltpu.make_async_copy(grad_ref, grads.at[place(0, 0)], grecv.at[place(0, 0)]).start()
    fetches = []
    for k, (dy, dx) in enumerate(ORDER):
        target = 2 * lax.rem(y_at + dy, 4) + lax.rem(x_at + dx, 2)
        at = pl.multiple_of((2 * target + core) * 512, 512)
        copy = pltpu.make_async_copy(
            froz_ref.at[:, :, pl.ds(at, 512)], weights.at[k, :, core], wsem.at[k]
        )
        copy.start()
        fetches.append(copy)
    meet(others)

    def token_slice(peer):
        at = pl.multiple_of((peer // 4) * BLOCK, BLOCK)
        start_row = pl.multiple_of(lax.rem(peer, 2) * ROWS, ROWS)
        return tok_ref.at[pl.ds(start_row, ROWS), pl.ds(at, BLOCK)]

    gather(grad_ref, place(3, 0), None, up)
    gather(grad_ref, place(1, 0), None, down)
    gather(grad_ref, place(0, 1), None, across)
    for k, peer in enumerate(others):
        go(push(token_slice(peer), x_scr.at[me], tsend.at[k], trecv.at[me], peer))
    pltpu.make_async_copy(token_slice(me), x_scr.at[me], trecv.at[me]).start()
    for k, (dy, dx) in enumerate(ORDER):
        target = 2 * lax.rem(y_at + dy, 4) + lax.rem(x_at + dx, 2)
        at = pl.multiple_of((2 * target + 1 - core) * 512, 512)
        go(push(
            froz_ref.at[:, :, pl.ds(at, 512)], weights.at[k, :, core], fsend.at[k], frecv.at[k], partner
        ))

    inverse_blocks(local_param, cross_param, inv_ref, rot)

    jobs = []
    for k in range(4):
        c = lax.rem(chip + k, 4)
        for side in range(2):
            jobs.append((
                rot.at[c, pl.ds(side * HALF, HALF), :], local.at[chip, core],
                lsend.at[k, side], lrecv.at[chip], 2 * (2 * c + side) + core, me,
            ))
    for level in range(4):
        bit, pair = pair_place(me, level)
        for k in range(4):
            c = lax.rem(chip + k, 4)
            jobs.append((
                rot.at[4 + 4 * level + c], cross.at[level, pair // 2, lax.rem(pair, 2)],
                send.at[level, k], recv.at[level, pair // 2],
                2 * (c + 4 * bit) + lax.rem(pair, 2), me,
            ))
    for job in jobs:
        start_job(*job)
    gathered(place(0, 1))
    gather(grads.at[place(0, 1)], place(3, 1), None, up)
    gather(grads.at[place(0, 1)], place(1, 1), None, down)
    gathered(place(3, 0))
    gather(grads.at[place(3, 0)], place(2, 0), 0, up)
    gathered(place(1, 0))
    gather(grads.at[place(1, 0)], place(2, 0), 1, down)

    def forward_on(stage):
        if stage == 0:
            for q in range(CHIPS):
                arrived(local.at[q, core], lrecv.at[q])
            part = local.at[:, core]
        else:
            for q in range(4):
                arrived(cross.at[stage - 1, q, core], recv.at[stage - 1, q])
            part = cross.at[stage - 1, :, core]
        go(push(part, part, psend.at[stage], precv.at[stage], partner))

    def weight(k):
        return weights[k].reshape(1024, 512)

    def cotangent(slot, first=False):
        fetches[slot].wait()
        arrived(weights.at[slot, :, 1 - core], frecv.at[slot])
        for rows, total_ref in ((other_row, theirs), (row, mine)):
            value = dot(grads[slot, pl.ds(rows, ROWS), :], weight(slot), NT)
            if first:
                total_ref[...] = value
            else:
                total_ref[...] += value

    forward_on(0)
    forward_on(1)
    for peer in [me] + others:
        arrived(x_scr.at[peer], trecv.at[peer])
    gathered(place(0, 0))
    cotangent(place(0, 0), True)
    arrived(local.at[:, 1 - core], precv.at[0])
    lanes = lax.broadcasted_iota(jnp.int32, (ROWS, BLOCK), 1)
    for m in range(CHIPS):
        parts = []
        for side in range(2):
            high, low = split(jnp.concatenate([local[m, side]] * 2, axis=0))
            x = x_scr[2 * m + side]
            parts.append(dot(x, high, NT) + dot(x, low, NT))
        saved[0, m // 2, :, (m % 2) * BLOCK:(m % 2 + 1) * BLOCK] = jnp.where(
            lanes < HALF, parts[0], parts[1]
        )
    for level in range(4):
        if level < 3:
            forward_on(level + 2)
        if level == 0:
            cotangent(place(0, 1))
            cotangent(place(3, 0))
        if level == 1:
            cotangent(place(1, 0))
        if level == 2:
            gathered(place(2, 0), 0)
            gathered(place(2, 0), 1)
            gather(grads.at[place(2, 0)], place(2, 1), None, across)
            cotangent(place(2, 0))
        arrived(cross.at[level, :, 1 - core], precv.at[level + 1])
        outs = []
        for index in range(4):
            one, two = pairs_of(level, index)
            a = cross[level, one // 2, one % 2]
            b = cross[level, two // 2, two % 2]
            matrix = split(place_near(a, b) if level % 2 == 0 else place_far(a, b))
            mats[level, index, 0] = matrix[0]
            mats[level, index, 1] = matrix[1]
            outs.append(dot3(split(saved[level, index]), matrix))
        if level % 2 == 1:
            outs = regroup(outs)
        for index in range(4):
            if level < 3:
                saved[level + 1, index] = outs[index]
            else:
                rotated[:, index * 256:(index + 1) * 256] = outs[index].astype(BF16)
    landing = act.at[pl.ds(row, ROWS), pl.ds(column, BLOCK)]
    for k, peer in enumerate(peers):
        source = pl.multiple_of((peer // 2) * BLOCK, BLOCK)
        go(push(rotated.at[:, pl.ds(source, BLOCK)], landing, asend.at[k], arecv.at[chip], peer))
    pltpu.make_async_copy(rotated.at[:, pl.ds(column, BLOCK)], landing, arecv.at[chip]).start()
    for slot in (place(3, 1), place(1, 1), place(2, 1)):
        gathered(slot)
        cotangent(slot)
    swap = push(theirs, landed, psend.at[5], precv.at[5], partner)
    swap.start()
    for peer in [me] + peers:
        at = pl.multiple_of((peer // 2) * BLOCK, BLOCK)
        arrived(act.at[pl.ds(row, ROWS), pl.ds(at, BLOCK)], arecv.at[peer // 2])
    part = act.at[pl.ds(row, ROWS), :]
    go(push(part, part, psend.at[6], precv.at[6], partner))
    swap.wait()
    rounded[...] = (mine[...] + landed[...]).astype(BF16)
    landing = rg.at[:, pl.ds(column, BLOCK)]
    for k, peer in enumerate(peers):
        source = pl.multiple_of((peer // 2) * BLOCK, BLOCK)
        go(push(rounded.at[:, pl.ds(source, BLOCK)], landing, rsend.at[k], rrecv.at[chip], peer))
    pltpu.make_async_copy(rounded.at[:, pl.ds(column, BLOCK)], landing, rrecv.at[chip]).start()
    arrived(act.at[pl.ds(other_row, ROWS), :], precv.at[6])

    def product(k, half):
        return dot(act[half * ROWS:(half + 1) * ROWS], weight(k))

    def give(slot, value, peer):
        sends_buf[slot] = value.astype(BF16)
        go(push(sends_buf.at[slot], lands.at[slot], osend.at[slot], orecv.at[slot], peer))

    def take(slot):
        arrived(lands.at[slot], orecv.at[slot])
        return lands[slot].astype(F32)

    for half in range(2):
        for k, peer in ((0, up), (1, down), (2, across)):
            give(2 * k + half, product(k, half), peer)
    give(8, product(4, 1), up)
    give(9, product(5, 0), down)
    for peer in [me] + peers:
        at = pl.multiple_of((peer // 2) * BLOCK, BLOCK)
        arrived(rg.at[:, pl.ds(at, BLOCK)], rrecv.at[peer // 2])

    state = [rg[:, index * 256:(index + 1) * 256].astype(F32) for index in range(4)]
    state = regroup(state)
    swaps = []
    for level in (3, 2, 1, 0):
        outs = []
        for index in range(4):
            grad = split(state[index])
            full = dot3(split(saved[level, index]), grad, TN)
            if level % 2 == 0:
                a, b = full[:BLOCK, :BLOCK], full[BLOCK:, BLOCK:]
            else:
                a, b = take_far(full)
            one, two = pairs_of(level, index)
            grad_cross[level, one % 2, one // 2] = a
            grad_cross[level, two % 2, two // 2] = b
            outs.append(dot3(grad, (mats[level, index, 0], mats[level, index, 1]), NT))
        state = regroup(outs) if level == 2 else outs
        copy = push(
            grad_cross.at[level, 1 - core], cross_in.at[level], bsend.at[level], brecv.at[level], partner
        )
        copy.start()
        swaps.append(copy)
        if level == 3:
            give(6, product(3, 0) + take(4), up)
            give(7, product(3, 1) + take(5), down)
        if level == 1:
            for half in range(2):
                give(12 + half, product(6, half) + (take(0 + half) + take(2 + half)), across)
    for m in range(CHIPS):
        grad = split(state[m // 2][:, (m % 2) * BLOCK:(m % 2 + 1) * BLOCK])
        for side in range(2):
            x = x_scr[2 * m + side]
            full = dot(grad[0], x, TN) + dot(grad[1], x, TN)
            grad_local[side, m] = full[side * HALF:(side + 1) * HALF]
    copy = push(grad_local.at[1 - core], local_in, bsend.at[4], brecv.at[4], partner)
    copy.start()
    swaps.append(copy)
    give(10, product(4, 0) + take(6), up)
    give(11, product(5, 1) + take(7), down)

    for level in (3, 2, 1, 0):
        swaps[3 - level].wait()
        cross_in[level] = cross_in[level] + grad_cross[level, core]
        slot = lax.rem(chip, 4)
        for k in range(4):
            q = lax.rem(chip + k, 4)
            job = (
                cross_in.at[level, q], own_ref.at[4 + 4 * level + slot],
                msend.at[level, k], mrecv.at[level, slot],
                pair_owner(2 * q + core, level, chip // 4), me,
            )
            start_job(*job)
            jobs.append(job)
    swaps[4].wait()
    local_in[...] = local_in[...] + grad_local[core]
    for k in range(CHIPS):
        q = lax.rem(chip + k, CHIPS)
        side = pl.multiple_of(lax.rem(chip, 2) * HALF, HALF)
        job = (
            local_in.at[q], own_ref.at[chip // 2, pl.ds(side, HALF), :],
            nsend.at[k], nrecv.at[chip], 2 * q + core, me,
        )
        start_job(*job)
        jobs.append(job)
    out_ref[0:ROWS] = product(7, 0) + (take(9) + take(12)) + take(10)
    out_ref[ROWS:] = product(7, 1) + (take(8) + take(13)) + take(11)
    for copy in sends:
        copy.wait_send()
    for job in jobs:
        drain_job(*job)
    for level in range(4):
        for c in range(4):
            arrived(own_ref.at[4 + 4 * level + c], mrecv.at[level, c])
    for g in range(CHIPS):
        arrived(own_ref.at[g // 2, pl.ds((g % 2) * HALF, HALF), :], nrecv.at[g])


def layer(tokens, frozen, grads, local_param, cross_param):
    return pl.pallas_call(
        layer_kernel,
        out_shape=(
            jax.ShapeDtypeStruct((512, 512), F32), jax.ShapeDtypeStruct((20, BLOCK, BLOCK), F32),
            jax.ShapeDtypeStruct((20, BLOCK, BLOCK), F32),
        ),
        in_specs=[ANY, ANY, ANY, VMEM, VMEM],
        out_specs=(VMEM, ANY, VMEM),
        scratch_shapes=[
            pltpu.VMEM((GROUP, ROWS, BLOCK), BF16), pltpu.VMEM((20, BLOCK, BLOCK), F32),
            pltpu.VMEM((4, 4, 2, BLOCK, BLOCK), F32), pltpu.VMEM((CHIPS, 2, HALF, BLOCK), F32),
            pltpu.VMEM((4, 4, 2, 256, 256), BF16), pltpu.VMEM((4, 4, ROWS, 256), F32),
            pltpu.VMEM((ROWS, 1024), BF16), pltpu.VMEM((512, 1024), BF16),
            pltpu.VMEM((CHIPS, CHIPS, 2, HALF, 512), BF16), pltpu.VMEM((CHIPS, 512, 512), BF16),
            pltpu.VMEM((14, ROWS, 512), BF16), pltpu.VMEM((14, ROWS, 512), BF16),
            pltpu.VMEM((ROWS, 1024), F32), pltpu.VMEM((ROWS, 1024), F32),
            pltpu.VMEM((ROWS, 1024), F32), pltpu.VMEM((ROWS, 1024), BF16),
            pltpu.VMEM((ROWS, 1024), BF16),
            pltpu.VMEM((4, 2, 4, BLOCK, BLOCK), F32), pltpu.VMEM((2, CHIPS, HALF, BLOCK), F32),
            pltpu.VMEM((4, 4, BLOCK, BLOCK), F32), pltpu.VMEM((CHIPS, HALF, BLOCK), F32),
            DMA((GROUP,)), DMA((GROUP,)), DMA((CHIPS,)), DMA((CHIPS,)), DMA((CHIPS,)),
            DMA((4, 4)), DMA((4, 4)), DMA((4, 2)), DMA((CHIPS,)), DMA((7,)), DMA((7,)),
            DMA((CHIPS,)), DMA((CHIPS,)), DMA((9,)), DMA((9,)), DMA((14,)), DMA((14,)),
            DMA((CHIPS,)), DMA((CHIPS,)), DMA((5,)), DMA((5,)), DMA((4, 4)), DMA((4, 4)),
            DMA((CHIPS,)), DMA((CHIPS,)),
        ],
        compiler_params=params_of(0),
    )(tokens, frozen.reshape(CHIPS, HALF, 8192), grads, local_param, cross_param)


def total_kernel(own_ref, out_ref, landed, part, send, recv, gsend, grecv):
    me = lax.axis_index("dp")
    others = [lax.rem(me + k, 8) for k in range(1, 8)]
    meet(others, "dp")
    copies = []
    for k, peer in enumerate(others):
        rows = own_ref.at[:, pl.ds(pl.multiple_of(peer * 16, 16), 16), :]
        copy = push(rows, landed.at[me], send.at[k], recv.at[me], peer, "dp")
        copy.start()
        copies.append(copy)
    mine = pl.ds(pl.multiple_of(me * 16, 16), 16)
    value = own_ref[:, mine, :]
    for peer in others:
        arrived(landed.at[peer], recv.at[peer])
        value = value + landed[peer]
    part[...] = value
    out_ref[:, mine, :] = value
    for k, peer in enumerate(others):
        copy = push(part, out_ref.at[:, mine, :], gsend.at[k], grecv.at[me], peer, "dp")
        copy.start()
        copies.append(copy)
    for peer in others:
        rows = out_ref.at[:, pl.ds(pl.multiple_of(peer * 16, 16), 16), :]
        arrived(rows, grecv.at[peer])
    for copy in copies:
        copy.wait_send()


def total(own):
    return pl.pallas_call(
        total_kernel,
        out_shape=jax.ShapeDtypeStruct((20, BLOCK, BLOCK), F32),
        in_specs=[VMEM],
        out_specs=VMEM,
        scratch_shapes=[
            pltpu.VMEM((8, 20, 16, BLOCK), F32), pltpu.VMEM((20, 16, BLOCK), F32),
            DMA((8,)), DMA((8,)), DMA((8,)), DMA((8,)),
        ],
        compiler_params=params_of(1),
    )(own)


def pull_many(inverse, matrix_grad):
    highest = lax.Precision.HIGHEST
    left = jnp.einsum("nji,njk->nik", inverse, matrix_grad, precision=highest)
    full = jnp.einsum("nik,njk->nij", left, inverse, precision=highest)
    return -2.0 * (full - full.transpose(0, 2, 1))


def body(tokens, frozen, local_param, cross_param, out_grad):
    output, own, inverse = layer(tokens, frozen, out_grad, local_param, cross_param)
    matrix_grad = total(own)
    matrix_grad = jnp.concatenate([matrix_grad[:4].transpose(0, 2, 1), matrix_grad[4:]])
    grads = pull_many(inverse, matrix_grad)
    return output, grads[:4], grads[4:].reshape(4, 4, BLOCK, BLOCK)


def solution(mesh):
    in_specs = (
        P("dp", "tensor"),
        P("tensor", None),
        P("tensor", None, None),
        P(None, "tensor", None, None),
        P("dp", "tensor"),
    )
    out_specs = (P("dp", "tensor"), P("tensor", None, None), P(None, "tensor", None, None))
    return jax.shard_map(body, mesh=mesh, in_specs=in_specs, out_specs=out_specs, check_vma=False)
```

```python
import jax
import jax.numpy as jnp
from jax import lax
from jax.experimental import pallas as pl
from jax.experimental.pallas import tpu as pltpu
from jax.sharding import PartitionSpec as P

MESH = pl.DeviceIdType.MESH
F32 = jnp.float32
BF16 = jnp.bfloat16
ANY = pl.BlockSpec(memory_space=pl.ANY)
VMEM = pl.BlockSpec(memory_space=pltpu.VMEM)
DMA = pltpu.SemaphoreType.DMA
GROUP = 16
CHIPS = 8
HALF = 64
BLOCK = 128
ROWS = 256


def params_of(identity, vmem=60):
    return pltpu.CompilerParams(
        collective_id=identity, has_side_effects=True, vmem_limit_bytes=vmem << 20
    )


def meet(peers, groups):
    barrier = pltpu.get_barrier_semaphore()
    for peer in peers:
        pl.semaphore_signal(barrier, inc=1, device_id={"tensor": peer}, device_id_type=MESH)
    for group in groups:
        pl.semaphore_signal(barrier, inc=1, device_id={"dp": group}, device_id_type=MESH)
    pl.semaphore_wait(barrier, len(peers) + len(groups))


def push(src, dst, send, recv, peer, axis="tensor"):
    return pltpu.make_async_remote_copy(
        src_ref=src, dst_ref=dst, send_sem=send, recv_sem=recv,
        device_id={axis: peer}, device_id_type=MESH,
    )


def start_job(src, dst, send, recv, peer, me):
    @pl.when(peer == me)
    def _():
        pltpu.make_async_copy(src, dst, recv).start()

    @pl.when(peer != me)
    def _():
        push(src, dst, send, recv, peer).start()


def drain_job(src, dst, send, recv, peer, me):
    @pl.when(peer != me)
    def _():
        push(src, dst, send, recv, peer).wait_send()


def arrived(ref, sem):
    pltpu.make_async_copy(ref, ref, sem).wait()


def split(value):
    high = value.astype(BF16)
    return high, (value - high.astype(F32)).astype(BF16)


def dot(a, b, dims=(((1,), (0,)), ((), ()))):
    return lax.dot_general(a, b, dims, preferred_element_type=F32)


NT = (((1,), (1,)), ((), ()))
TN = (((0,), (0,)), ((), ()))


def dot3(a, b, dims=(((1,), (0,)), ((), ()))):
    return dot(a[0], b[0], dims) + (dot(a[0], b[1], dims) + dot(a[1], b[0], dims))


def inverse_blocks(local_param, cross_param, out_ref, rot_ref):
    count, size, _ = out_ref.shape
    step = 32
    rows = lax.broadcasted_iota(jnp.int32, (size, size), 0)
    lanes = lax.broadcasted_iota(jnp.int32, (size, size), 1)
    panel_rows = lax.broadcasted_iota(jnp.int32, (step, size), 0)
    panel_lanes = lax.broadcasted_iota(jnp.int32, (step, size), 1)
    identity = jnp.where(rows == lanes, 1.0, 0.0)
    for at in range(count):
        param = local_param[at] if at < 4 else cross_param[(at - 4) // 4, at % 4]
        out_ref[at] = identity + param - param.T

    def eliminate(block_at, carry):
        start = pl.multiple_of(block_at * step, step)
        shift = lax.rem(size - start, size)
        inside = (lanes >= start) & (lanes < start + step)
        panels = [pltpu.roll(out_ref[at, pl.ds(start, step), :], shift, 1) for at in range(count)]
        for k in range(step):
            for at in range(count):
                panel = panels[at]
                column = panel[:, k:k + 1]
                scale = 1.0 / panel[k:k + 1, k:k + 1]
                row = jnp.where(panel_lanes[:1] == k, 1.0, panel[k:k + 1, :]) * scale
                rest = jnp.where(panel_lanes == k, 0.0, panel) - column * row
                panels[at] = jnp.where(panel_rows == k, row, rest)
        panels = [pltpu.roll(panel, start, 1) for panel in panels]
        for at in range(count):
            matrix = out_ref[at]
            turned = pltpu.roll(matrix, shift, 1)[:, :step]
            out_ref[at] = jnp.where(inside, 0.0, matrix) - jnp.dot(
                turned, panels[at], precision=lax.Precision.HIGHEST, preferred_element_type=F32
            )
        for at in range(count):
            out_ref[at, pl.ds(start, step), :] = panels[at]
        return carry

    lax.fori_loop(0, size // step, eliminate, 0)
    for at in range(count):
        rotation = 2.0 * out_ref[at] - identity
        rot_ref[at] = rotation.T if at < 4 else rotation


def pair_place(me, level):
    low = 2 ** level
    bit = lax.rem(me // low, 2)
    pair = (me // (2 * low)) * low + lax.rem(me, low)
    return bit, pair


def pair_owner(pair, level, bit):
    low = 2 ** level
    return (pair // low) * (2 * low) + bit * low + lax.rem(pair, low)


def mix(a, b, r):
    at = (r // 2) * BLOCK
    first, second = a[:, at:at + BLOCK], b[:, at:at + BLOCK]
    lanes = lax.broadcasted_iota(jnp.int32, first.shape, 1)
    if r % 2 == 0:
        return jnp.where(lanes < HALF, first, pltpu.roll(second, HALF, 1))
    return jnp.where(lanes < HALF, pltpu.roll(first, HALF, 1), second)


def regroup(quads):
    return [
        jnp.concatenate([mix(quads[0], quads[1], r), mix(quads[2], quads[3], r)], axis=1)
        for r in range(4)
    ]


def place_near(a, b):
    zero = jnp.zeros((BLOCK, BLOCK), F32)
    return jnp.concatenate(
        [jnp.concatenate([a, zero], axis=1), jnp.concatenate([zero, b], axis=1)], axis=0
    )


def place_far(a, b):
    lanes = lax.broadcasted_iota(jnp.int32, (BLOCK, BLOCK), 1)
    turned_a, turned_b = pltpu.roll(a, HALF, 1), pltpu.roll(b, HALF, 1)
    low = lanes < HALF
    a_rows = jnp.concatenate([jnp.where(low, a, 0.0), jnp.where(low, turned_a, 0.0)], axis=1)
    b_rows = jnp.concatenate([jnp.where(low, 0.0, turned_b), jnp.where(low, 0.0, b)], axis=1)
    return jnp.concatenate(
        [a_rows[:HALF], b_rows[:HALF], a_rows[HALF:], b_rows[HALF:]], axis=0
    )


def take_far(full):
    lanes = lax.broadcasted_iota(jnp.int32, (BLOCK, BLOCK), 1)
    low = lanes < HALF
    a_rows = jnp.concatenate([full[:HALF], full[BLOCK:BLOCK + HALF]], axis=0)
    b_rows = jnp.concatenate([full[HALF:BLOCK], full[BLOCK + HALF:]], axis=0)
    a = jnp.where(low, a_rows[:, :BLOCK], pltpu.roll(a_rows[:, BLOCK:], HALF, 1))
    b = jnp.where(low, pltpu.roll(b_rows[:, :BLOCK], HALF, 1), b_rows[:, BLOCK:])
    return a, b


def pairs_of(level, index):
    if level < 2:
        return 2 * index, 2 * index + 1
    return index, 4 + index


ORDER = [(1, 1), (3, 1), (2, 1), (2, 0), (1, 0), (3, 0), (0, 1), (0, 0)]


def layer_kernel(
    tok_ref, froz_ref, grad_ref, local_param, cross_param,
    out_ref, local_out, cross_out,
    x_scr, rot, cross, local, mats, saved, rotated, act, weights, grads, sends_buf, lands,
    mine, theirs, landed, rounded, rg, grad_cross, grad_local, cross_in, local_in,
    total_ref, inv_ref, own, z_send, z_land, z_sum, side_land,
    tsend, trecv, fsend, frecv, wsem, send, recv, lsend, lrecv, psend, precv, asend, arecv,
    gsend, grecv, osend, orecv, rsend, rrecv, bsend, brecv, msend, mrecv, nsend, nrecv, zsend, zrecv,
):
    me = lax.axis_index("tensor")
    core = lax.rem(me, 2)
    chip = me // 2
    partner = me + 1 - 2 * core
    x_at, y_at = lax.rem(chip, 2), chip // 2
    across = 2 * (chip + 1 - 2 * x_at) + core
    up = 2 * lax.rem(chip + 2, CHIPS) + core
    down = 2 * lax.rem(chip + 6, CHIPS) + core
    others = [lax.rem(me + k, GROUP) for k in range(1, GROUP)]
    peers = [lax.rem(me + 2 * k, GROUP) for k in range(1, CHIPS)]
    row = pl.multiple_of(core * ROWS, ROWS)
    other_row = pl.multiple_of((1 - core) * ROWS, ROWS)
    column = pl.multiple_of(chip * BLOCK, BLOCK)
    sends = []

    def go(copy):
        copy.start()
        sends.append(copy)

    def place(dy, dx):
        return ORDER.index((dy, dx))

    def gather(src, slot, half, peer):
        part = src if half is None else src.at[pl.ds(half * ROWS, ROWS), :]
        dst = grads.at[slot] if half is None else grads.at[slot, pl.ds(half * ROWS, ROWS), :]
        at = len(ORDER) if half == 1 else slot
        go(push(part, dst, gsend.at[at], grecv.at[at], peer))

    def gathered(slot, half=None):
        dst = grads.at[slot] if half is None else grads.at[slot, pl.ds(half * ROWS, ROWS), :]
        arrived(dst, grecv.at[len(ORDER) if half == 1 else slot])

    pltpu.make_async_copy(grad_ref, grads.at[place(0, 0)], grecv.at[place(0, 0)]).start()
    fetches = []
    for k, (dy, dx) in enumerate(ORDER):
        target = 2 * lax.rem(y_at + dy, 4) + lax.rem(x_at + dx, 2)
        at = pl.multiple_of((2 * target + core) * 512, 512)
        copy = pltpu.make_async_copy(
            froz_ref.at[:, :, pl.ds(at, 512)], weights.at[k, :, core], wsem.at[k]
        )
        copy.start()
        fetches.append(copy)
    batch = lax.axis_index("dp")
    z_at, side_at = batch // 2, lax.rem(batch, 2)
    z_peers = [lax.rem(z_at + k, 4) for k in range(1, 4)]
    side_peer = 2 * z_at + 1 - side_at
    meet(others, [2 * z + side_at for z in z_peers] + [side_peer])

    def token_slice(peer):
        at = pl.multiple_of((peer // 4) * BLOCK, BLOCK)
        start_row = pl.multiple_of(lax.rem(peer, 2) * ROWS, ROWS)
        return tok_ref.at[pl.ds(start_row, ROWS), pl.ds(at, BLOCK)]

    gather(grad_ref, place(3, 0), None, up)
    gather(grad_ref, place(1, 0), None, down)
    gather(grad_ref, place(0, 1), None, across)
    for k, peer in enumerate(others):
        go(push(token_slice(peer), x_scr.at[me], tsend.at[k], trecv.at[me], peer))
    pltpu.make_async_copy(token_slice(me), x_scr.at[me], trecv.at[me]).start()
    for k, (dy, dx) in enumerate(ORDER):
        target = 2 * lax.rem(y_at + dy, 4) + lax.rem(x_at + dx, 2)
        at = pl.multiple_of((2 * target + 1 - core) * 512, 512)
        go(push(
            froz_ref.at[:, :, pl.ds(at, 512)], weights.at[k, :, core], fsend.at[k], frecv.at[k], partner
        ))

    inverse_blocks(local_param, cross_param, inv_ref, rot)

    jobs = []
    for k in range(4):
        c = lax.rem(chip + k, 4)
        for side in range(2):
            jobs.append((
                rot.at[c, pl.ds(side * HALF, HALF), :], local.at[chip, core],
                lsend.at[k, side], lrecv.at[chip], 2 * (2 * c + side) + core, me,
            ))
    for level in range(4):
        bit, pair = pair_place(me, level)
        for k in range(4):
            c = lax.rem(chip + k, 4)
            jobs.append((
                rot.at[4 + 4 * level + c], cross.at[level, pair // 2, lax.rem(pair, 2)],
                send.at[level, k], recv.at[level, pair // 2],
                2 * (c + 4 * bit) + lax.rem(pair, 2), me,
            ))
    gathered(place(3, 0))
    gather(grads.at[place(3, 0)], place(2, 0), 0, up)
    gathered(place(1, 0))
    gather(grads.at[place(1, 0)], place(2, 0), 1, down)
    for job in jobs:
        start_job(*job)
    gathered(place(0, 1))
    gather(grads.at[place(0, 1)], place(3, 1), None, up)
    gather(grads.at[place(0, 1)], place(1, 1), None, down)

    def forward_on(stage):
        if stage == 0:
            for q in range(CHIPS):
                arrived(local.at[q, core], lrecv.at[q])
            part = local.at[:, core]
        else:
            for q in range(4):
                arrived(cross.at[stage - 1, q, core], recv.at[stage - 1, q])
            part = cross.at[stage - 1, :, core]
        go(push(part, part, psend.at[stage], precv.at[stage], partner))

    def weight(k):
        return weights[k].reshape(1024, 512)

    def cotangent(slot, first=False):
        fetches[slot].wait()
        arrived(weights.at[slot, :, 1 - core], frecv.at[slot])
        for rows, total_ref in ((other_row, theirs), (row, mine)):
            value = dot(grads[slot, pl.ds(rows, ROWS), :], weight(slot), NT)
            if first:
                total_ref[...] = value
            else:
                total_ref[...] += value

    forward_on(0)
    forward_on(1)
    for peer in [me] + others:
        arrived(x_scr.at[peer], trecv.at[peer])
    gathered(place(0, 0))
    cotangent(place(0, 0), True)
    arrived(local.at[:, 1 - core], precv.at[0])
    lanes = lax.broadcasted_iota(jnp.int32, (ROWS, BLOCK), 1)
    for m in range(CHIPS):
        parts = []
        for side in range(2):
            high, low = split(jnp.concatenate([local[m, side]] * 2, axis=0))
            x = x_scr[2 * m + side]
            parts.append(dot(x, high, NT) + dot(x, low, NT))
        saved[0, m // 2, :, (m % 2) * BLOCK:(m % 2 + 1) * BLOCK] = jnp.where(
            lanes < HALF, parts[0], parts[1]
        )
    for level in range(4):
        if level < 3:
            forward_on(level + 2)
        if level == 0:
            gathered(place(2, 0), 0)
            gathered(place(2, 0), 1)
            gather(grads.at[place(2, 0)], place(2, 1), None, across)
            cotangent(place(0, 1))
            cotangent(place(3, 0))
        if level == 1:
            cotangent(place(1, 0))
        if level == 2:
            cotangent(place(2, 0))
        arrived(cross.at[level, :, 1 - core], precv.at[level + 1])
        outs = []
        for index in range(4):
            one, two = pairs_of(level, index)
            a = cross[level, one // 2, one % 2]
            b = cross[level, two // 2, two % 2]
            matrix = split(place_near(a, b) if level % 2 == 0 else place_far(a, b))
            mats[level, index, 0] = matrix[0]
            mats[level, index, 1] = matrix[1]
            outs.append(dot3(split(saved[level, index]), matrix))
        if level % 2 == 1:
            outs = regroup(outs)
        for index in range(4):
            if level < 3:
                saved[level + 1, index] = outs[index]
            else:
                rotated[:, index * 256:(index + 1) * 256] = outs[index].astype(BF16)
    landing = act.at[pl.ds(row, ROWS), pl.ds(column, BLOCK)]
    for k, peer in enumerate(peers):
        source = pl.multiple_of((peer // 2) * BLOCK, BLOCK)
        go(push(rotated.at[:, pl.ds(source, BLOCK)], landing, asend.at[k], arecv.at[chip], peer))
    pltpu.make_async_copy(rotated.at[:, pl.ds(column, BLOCK)], landing, arecv.at[chip]).start()
    for slot in (place(3, 1), place(1, 1), place(2, 1)):
        gathered(slot)
        cotangent(slot)
    swap = push(theirs, landed, psend.at[5], precv.at[5], partner)
    swap.start()
    for peer in [me] + peers:
        at = pl.multiple_of((peer // 2) * BLOCK, BLOCK)
        arrived(act.at[pl.ds(row, ROWS), pl.ds(at, BLOCK)], arecv.at[peer // 2])
    part = act.at[pl.ds(row, ROWS), :]
    go(push(part, part, psend.at[6], precv.at[6], partner))
    swap.wait()
    rounded[...] = (mine[...] + landed[...]).astype(BF16)
    landing = rg.at[:, pl.ds(column, BLOCK)]
    for k, peer in enumerate(peers):
        source = pl.multiple_of((peer // 2) * BLOCK, BLOCK)
        go(push(rounded.at[:, pl.ds(source, BLOCK)], landing, rsend.at[k], rrecv.at[chip], peer))
    pltpu.make_async_copy(rounded.at[:, pl.ds(column, BLOCK)], landing, rrecv.at[chip]).start()
    arrived(act.at[pl.ds(other_row, ROWS), :], precv.at[6])

    def product(k, half):
        return dot(act[half * ROWS:(half + 1) * ROWS], weight(k))

    def ready(slot, value):
        sends_buf[slot] = value.astype(BF16)

    def give(slot, value, peer):
        ready(slot, value)
        go(push(sends_buf.at[slot], lands.at[slot], osend.at[slot], orecv.at[slot], peer))

    def take(slot):
        arrived(lands.at[slot], orecv.at[slot])
        return lands[slot].astype(F32)

    for peer in [me] + peers:
        at = pl.multiple_of((peer // 2) * BLOCK, BLOCK)
        arrived(rg.at[:, pl.ds(at, BLOCK)], rrecv.at[peer // 2])

    state = [rg[:, index * 256:(index + 1) * 256].astype(F32) for index in range(4)]
    state = regroup(state)
    swaps = []
    for level in (3, 2, 1, 0):
        outs = []
        for index in range(4):
            grad = split(state[index])
            full = dot3(split(saved[level, index]), grad, TN)
            if level % 2 == 0:
                a, b = full[:BLOCK, :BLOCK], full[BLOCK:, BLOCK:]
            else:
                a, b = take_far(full)
            one, two = pairs_of(level, index)
            grad_cross[level, one % 2, one // 2] = a
            grad_cross[level, two % 2, two // 2] = b
            outs.append(dot3(grad, (mats[level, index, 0], mats[level, index, 1]), NT))
        state = regroup(outs) if level == 2 else outs
        copy = push(
            grad_cross.at[level, 1 - core], cross_in.at[level], bsend.at[level], brecv.at[level], partner
        )
        copy.start()
        swaps.append(copy)
    for m in range(CHIPS):
        grad = split(state[m // 2][:, (m % 2) * BLOCK:(m % 2 + 1) * BLOCK])
        for side in range(2):
            x = x_scr[2 * m + side]
            full = dot(grad[0], x, TN) + dot(grad[1], x, TN)
            grad_local[side, m] = full[side * HALF:(side + 1) * HALF]
    copy = push(grad_local.at[1 - core], local_in, bsend.at[4], brecv.at[4], partner)
    copy.start()
    swaps.append(copy)
    for level in (3, 2, 1, 0):
        swaps[3 - level].wait()
        cross_in[level] = cross_in[level] + grad_cross[level, core]
        slot = lax.rem(chip, 4)
        for k in range(4):
            q = lax.rem(chip + k, 4)
            job = (
                cross_in.at[level, q], own.at[4 + 4 * level + slot],
                msend.at[level, k], mrecv.at[level, slot],
                pair_owner(2 * q + core, level, chip // 4), me,
            )
            start_job(*job)
            jobs.append(job)
    swaps[4].wait()
    local_in[...] = local_in[...] + grad_local[core]
    for k in range(CHIPS):
        q = lax.rem(chip + k, CHIPS)
        side = pl.multiple_of(lax.rem(chip, 2) * HALF, HALF)
        job = (
            local_in.at[q], own.at[chip // 2, pl.ds(side, HALF), :],
            nsend.at[k], nrecv.at[chip], 2 * q + core, me,
        )
        start_job(*job)
        jobs.append(job)
    for half in range(2):
        for k in range(3):
            ready(2 * k + half, product(k, half))
    for level in range(4):
        for c in range(4):
            arrived(own.at[4 + 4 * level + c], mrecv.at[level, c])
    for g in range(CHIPS):
        arrived(own.at[g // 2, pl.ds((g % 2) * HALF, HALF), :], nrecv.at[g])
    own_rows = pl.ds(pl.multiple_of(z_at * 32, 32), 32)
    for k, z in enumerate(z_peers):
        z_send[k] = own[:, pl.ds(pl.multiple_of(z * 32, 32), 32), :].astype(BF16)
        go(push(z_send.at[k], z_land.at[z_at], zsend.at[k], zrecv.at[z_at], 2 * z + side_at, "dp"))
    for half in range(2):
        for k, peer in ((0, up), (1, down), (2, across)):
            slot = 2 * k + half
            go(push(sends_buf.at[slot], lands.at[slot], osend.at[slot], orecv.at[slot], peer))
    give(8, product(4, 1), up)
    give(9, product(5, 0), down)
    value = own[:, own_rows, :]
    for z in z_peers:
        arrived(z_land.at[z], zrecv.at[z])
        value = value + z_land[z].astype(F32)
    z_sum[...] = value
    their_part = pl.ds(pl.multiple_of((1 - side_at) * 16, 16), 16)
    my_part = pl.ds(pl.multiple_of(side_at * 16, 16), 16)
    go(push(z_sum.at[:, their_part, :], side_land, zsend.at[3], zrecv.at[4], side_peer, "dp"))
    give(6, product(3, 0) + take(4), up)
    give(7, product(3, 1) + take(5), down)
    for half in range(2):
        give(12 + half, product(6, half) + (take(0 + half) + take(2 + half)), across)
    arrived(side_land, zrecv.at[4])
    my_rows = pl.ds(pl.multiple_of(z_at * 32 + side_at * 16, 16), 16)
    their_rows = pl.ds(pl.multiple_of(z_at * 32 + (1 - side_at) * 16, 16), 16)
    total_ref[:, my_rows, :] = z_sum[:, my_part, :] + side_land[...]
    mine_rows = total_ref.at[:, my_rows, :]
    go(push(mine_rows, mine_rows, zsend.at[4], zrecv.at[5], side_peer, "dp"))
    give(10, product(4, 0) + take(6), up)
    give(11, product(5, 1) + take(7), down)
    arrived(total_ref.at[:, their_rows, :], zrecv.at[5])
    both = total_ref.at[:, own_rows, :]
    for k, z in enumerate(z_peers):
        go(push(both, both, zsend.at[5 + k], zrecv.at[6 + z_at], 2 * z + side_at, "dp"))
    out_ref[0:ROWS] = product(7, 0) + (take(9) + take(12)) + take(10)
    out_ref[ROWS:] = product(7, 1) + (take(8) + take(13)) + take(11)
    for z in z_peers:
        arrived(total_ref.at[:, pl.ds(pl.multiple_of(z * 32, 32), 32), :], zrecv.at[6 + z])
    for at in range(20):
        matrix = total_ref[at].T if at < 4 else total_ref[at]
        inverse = split(inv_ref[at])
        left = dot3(inverse, split(matrix), TN)
        full = dot3(split(left), inverse, NT)
        pulled = -2.0 * (full - full.T)
        if at < 4:
            local_out[at] = pulled
        else:
            cross_out[(at - 4) // 4, at % 4] = pulled
    for copy in sends:
        copy.wait_send()
    for job in jobs:
        drain_job(*job)


def layer(tokens, frozen, grads, local_param, cross_param):
    return pl.pallas_call(
        layer_kernel,
        out_shape=(
            jax.ShapeDtypeStruct((512, 512), F32), jax.ShapeDtypeStruct((4, BLOCK, BLOCK), F32),
            jax.ShapeDtypeStruct((4, 4, BLOCK, BLOCK), F32),
        ),
        in_specs=[ANY, ANY, ANY, VMEM, VMEM],
        out_specs=(VMEM, VMEM, VMEM),
        scratch_shapes=[
            pltpu.VMEM((GROUP, ROWS, BLOCK), BF16), pltpu.VMEM((20, BLOCK, BLOCK), F32),
            pltpu.VMEM((4, 4, 2, BLOCK, BLOCK), F32), pltpu.VMEM((CHIPS, 2, HALF, BLOCK), F32),
            pltpu.VMEM((4, 4, 2, 256, 256), BF16), pltpu.VMEM((4, 4, ROWS, 256), F32),
            pltpu.VMEM((ROWS, 1024), BF16), pltpu.VMEM((512, 1024), BF16),
            pltpu.VMEM((CHIPS, CHIPS, 2, HALF, 512), BF16), pltpu.VMEM((CHIPS, 512, 512), BF16),
            pltpu.VMEM((14, ROWS, 512), BF16), pltpu.VMEM((14, ROWS, 512), BF16),
            pltpu.VMEM((ROWS, 1024), F32), pltpu.VMEM((ROWS, 1024), F32),
            pltpu.VMEM((ROWS, 1024), F32), pltpu.VMEM((ROWS, 1024), BF16),
            pltpu.VMEM((ROWS, 1024), BF16),
            pltpu.VMEM((4, 2, 4, BLOCK, BLOCK), F32), pltpu.VMEM((2, CHIPS, HALF, BLOCK), F32),
            pltpu.VMEM((4, 4, BLOCK, BLOCK), F32), pltpu.VMEM((CHIPS, HALF, BLOCK), F32),
            pltpu.VMEM((20, BLOCK, BLOCK), F32), pltpu.VMEM((20, BLOCK, BLOCK), F32),
            pltpu.VMEM((20, BLOCK, BLOCK), F32), pltpu.VMEM((3, 20, 32, BLOCK), BF16),
            pltpu.VMEM((4, 20, 32, BLOCK), BF16), pltpu.VMEM((20, 32, BLOCK), F32),
            pltpu.VMEM((20, 16, BLOCK), F32),
            DMA((GROUP,)), DMA((GROUP,)), DMA((CHIPS,)), DMA((CHIPS,)), DMA((CHIPS,)),
            DMA((4, 4)), DMA((4, 4)), DMA((4, 2)), DMA((CHIPS,)), DMA((7,)), DMA((7,)),
            DMA((CHIPS,)), DMA((CHIPS,)), DMA((9,)), DMA((9,)), DMA((14,)), DMA((14,)),
            DMA((CHIPS,)), DMA((CHIPS,)), DMA((5,)), DMA((5,)), DMA((4, 4)), DMA((4, 4)),
            DMA((CHIPS,)), DMA((CHIPS,)), DMA((8,)), DMA((10,)),
        ],
        compiler_params=params_of(0),
    )(tokens, frozen.reshape(CHIPS, HALF, 8192), grads, local_param, cross_param)


def body(tokens, frozen, local_param, cross_param, out_grad):
    return layer(tokens, frozen, out_grad, local_param, cross_param)


def solution(mesh):
    in_specs = (
        P("dp", "tensor"),
        P("tensor", None),
        P("tensor", None, None),
        P(None, "tensor", None, None),
        P("dp", "tensor"),
    )
    out_specs = (P("dp", "tensor"), P("tensor", None, None), P(None, "tensor", None, None))
    return jax.shard_map(body, mesh=mesh, in_specs=in_specs, out_specs=out_specs, check_vma=False)
```

```python
import jax
import jax.numpy as jnp
from jax import lax
from jax.experimental import pallas as pl
from jax.experimental.pallas import tpu as pltpu
from jax.sharding import PartitionSpec as P

MESH = pl.DeviceIdType.MESH
F32 = jnp.float32
BF16 = jnp.bfloat16
ANY = pl.BlockSpec(memory_space=pl.ANY)
VMEM = pl.BlockSpec(memory_space=pltpu.VMEM)
DMA = pltpu.SemaphoreType.DMA
GROUP = 16
CHIPS = 8
HALF = 64
BLOCK = 128
ROWS = 256


def params_of(identity, vmem=60):
    return pltpu.CompilerParams(
        collective_id=identity, has_side_effects=True, vmem_limit_bytes=vmem << 20
    )


def meet(peers, groups):
    barrier = pltpu.get_barrier_semaphore()
    for peer in peers:
        pl.semaphore_signal(barrier, inc=1, device_id={"tensor": peer}, device_id_type=MESH)
    for group in groups:
        pl.semaphore_signal(barrier, inc=1, device_id={"dp": group}, device_id_type=MESH)
    pl.semaphore_wait(barrier, len(peers) + len(groups))


def push(src, dst, send, recv, peer, axis="tensor"):
    return pltpu.make_async_remote_copy(
        src_ref=src, dst_ref=dst, send_sem=send, recv_sem=recv,
        device_id={axis: peer}, device_id_type=MESH,
    )


def start_job(src, dst, send, recv, peer, me):
    @pl.when(peer == me)
    def _():
        pltpu.make_async_copy(src, dst, recv).start()

    @pl.when(peer != me)
    def _():
        push(src, dst, send, recv, peer).start()


def drain_job(src, dst, send, recv, peer, me):
    @pl.when(peer != me)
    def _():
        push(src, dst, send, recv, peer).wait_send()


def arrived(ref, sem):
    pltpu.make_async_copy(ref, ref, sem).wait()


def split(value):
    high = value.astype(BF16)
    return high, (value - high.astype(F32)).astype(BF16)


def dot(a, b, dims=(((1,), (0,)), ((), ()))):
    return lax.dot_general(a, b, dims, preferred_element_type=F32)


NT = (((1,), (1,)), ((), ()))
TN = (((0,), (0,)), ((), ()))


def dot3(a, b, dims=(((1,), (0,)), ((), ()))):
    return dot(a[0], b[0], dims) + (dot(a[0], b[1], dims) + dot(a[1], b[0], dims))


def inverse_blocks(local_param, cross_param, out_ref, rot_ref):
    count, size, _ = out_ref.shape
    step = 32
    rows = lax.broadcasted_iota(jnp.int32, (size, size), 0)
    lanes = lax.broadcasted_iota(jnp.int32, (size, size), 1)
    panel_rows = lax.broadcasted_iota(jnp.int32, (step, size), 0)
    panel_lanes = lax.broadcasted_iota(jnp.int32, (step, size), 1)
    identity = jnp.where(rows == lanes, 1.0, 0.0)
    for at in range(count):
        param = local_param[at] if at < 4 else cross_param[(at - 4) // 4, at % 4]
        out_ref[at] = identity + param - param.T

    def eliminate(block_at, carry):
        start = pl.multiple_of(block_at * step, step)
        shift = lax.rem(size - start, size)
        inside = (lanes >= start) & (lanes < start + step)
        panels = [pltpu.roll(out_ref[at, pl.ds(start, step), :], shift, 1) for at in range(count)]
        for k in range(step):
            for at in range(count):
                panel = panels[at]
                column = panel[:, k:k + 1]
                scale = 1.0 / panel[k:k + 1, k:k + 1]
                row = jnp.where(panel_lanes[:1] == k, 1.0, panel[k:k + 1, :]) * scale
                rest = jnp.where(panel_lanes == k, 0.0, panel) - column * row
                panels[at] = jnp.where(panel_rows == k, row, rest)
        panels = [pltpu.roll(panel, start, 1) for panel in panels]
        for at in range(count):
            matrix = out_ref[at]
            turned = pltpu.roll(matrix, shift, 1)[:, :step]
            out_ref[at] = jnp.where(inside, 0.0, matrix) - jnp.dot(
                turned, panels[at], precision=lax.Precision.HIGHEST, preferred_element_type=F32
            )
        for at in range(count):
            out_ref[at, pl.ds(start, step), :] = panels[at]
        return carry

    lax.fori_loop(0, size // step, eliminate, 0)
    for at in range(count):
        rotation = 2.0 * out_ref[at] - identity
        rot_ref[at] = rotation.T if at < 4 else rotation


def pair_place(me, level):
    low = 2 ** level
    bit = lax.rem(me // low, 2)
    pair = (me // (2 * low)) * low + lax.rem(me, low)
    return bit, pair


def pair_owner(pair, level, bit):
    low = 2 ** level
    return (pair // low) * (2 * low) + bit * low + lax.rem(pair, low)


def mix(a, b, r):
    at = (r // 2) * BLOCK
    first, second = a[:, at:at + BLOCK], b[:, at:at + BLOCK]
    lanes = lax.broadcasted_iota(jnp.int32, first.shape, 1)
    if r % 2 == 0:
        return jnp.where(lanes < HALF, first, pltpu.roll(second, HALF, 1))
    return jnp.where(lanes < HALF, pltpu.roll(first, HALF, 1), second)


def regroup(quads):
    return [
        jnp.concatenate([mix(quads[0], quads[1], r), mix(quads[2], quads[3], r)], axis=1)
        for r in range(4)
    ]


def place_near(a, b):
    zero = jnp.zeros((BLOCK, BLOCK), F32)
    return jnp.concatenate(
        [jnp.concatenate([a, zero], axis=1), jnp.concatenate([zero, b], axis=1)], axis=0
    )


def place_far(a, b):
    lanes = lax.broadcasted_iota(jnp.int32, (BLOCK, BLOCK), 1)
    turned_a, turned_b = pltpu.roll(a, HALF, 1), pltpu.roll(b, HALF, 1)
    low = lanes < HALF
    a_rows = jnp.concatenate([jnp.where(low, a, 0.0), jnp.where(low, turned_a, 0.0)], axis=1)
    b_rows = jnp.concatenate([jnp.where(low, 0.0, turned_b), jnp.where(low, 0.0, b)], axis=1)
    return jnp.concatenate(
        [a_rows[:HALF], b_rows[:HALF], a_rows[HALF:], b_rows[HALF:]], axis=0
    )


def take_far(full):
    lanes = lax.broadcasted_iota(jnp.int32, (BLOCK, BLOCK), 1)
    low = lanes < HALF
    a_rows = jnp.concatenate([full[:HALF], full[BLOCK:BLOCK + HALF]], axis=0)
    b_rows = jnp.concatenate([full[HALF:BLOCK], full[BLOCK + HALF:]], axis=0)
    a = jnp.where(low, a_rows[:, :BLOCK], pltpu.roll(a_rows[:, BLOCK:], HALF, 1))
    b = jnp.where(low, pltpu.roll(b_rows[:, :BLOCK], HALF, 1), b_rows[:, BLOCK:])
    return a, b


def pairs_of(level, index):
    if level < 2:
        return 2 * index, 2 * index + 1
    return index, 4 + index


ORDER = [(1, 1), (3, 1), (2, 1), (2, 0), (1, 0), (3, 0), (0, 1), (0, 0)]


def layer_kernel(
    tok_ref, froz_ref, grad_ref, local_param, cross_param,
    out_ref, local_out, cross_out,
    x_scr, rot, cross, local, mats, saved, rotated, act, weights, grads, sends_buf, lands,
    mine, theirs, landed, rounded, rg, grad_cross, grad_local, cross_in, local_in,
    total_ref, inv_ref, own, z_send, z_land, z_sum, side_land,
    tsend, trecv, fsend, frecv, wsem, send, recv, lsend, lrecv, psend, precv, asend, arecv,
    gsend, grecv, osend, orecv, rsend, rrecv, bsend, brecv, msend, mrecv, nsend, nrecv, zsend, zrecv,
):
    me = lax.axis_index("tensor")
    core = lax.rem(me, 2)
    chip = me // 2
    partner = me + 1 - 2 * core
    x_at, y_at = lax.rem(chip, 2), chip // 2
    across = 2 * (chip + 1 - 2 * x_at) + core
    up = 2 * lax.rem(chip + 2, CHIPS) + core
    down = 2 * lax.rem(chip + 6, CHIPS) + core
    others = [lax.rem(me + k, GROUP) for k in range(1, GROUP)]
    peers = [lax.rem(me + 2 * k, GROUP) for k in range(1, CHIPS)]
    row = pl.multiple_of(core * ROWS, ROWS)
    other_row = pl.multiple_of((1 - core) * ROWS, ROWS)
    column = pl.multiple_of(chip * BLOCK, BLOCK)
    sends = []

    def go(copy):
        copy.start()
        sends.append(copy)

    def place(dy, dx):
        return ORDER.index((dy, dx))

    def gather(src, slot, half, peer):
        part = src if half is None else src.at[pl.ds(half * ROWS, ROWS), :]
        dst = grads.at[slot] if half is None else grads.at[slot, pl.ds(half * ROWS, ROWS), :]
        at = len(ORDER) if half == 1 else slot
        go(push(part, dst, gsend.at[at], grecv.at[at], peer))

    def gathered(slot, half=None):
        dst = grads.at[slot] if half is None else grads.at[slot, pl.ds(half * ROWS, ROWS), :]
        arrived(dst, grecv.at[len(ORDER) if half == 1 else slot])

    pltpu.make_async_copy(grad_ref, grads.at[place(0, 0)], grecv.at[place(0, 0)]).start()
    fetches = []
    for k, (dy, dx) in enumerate(ORDER):
        target = 2 * lax.rem(y_at + dy, 4) + lax.rem(x_at + dx, 2)
        at = pl.multiple_of((2 * target + core) * 512, 512)
        copy = pltpu.make_async_copy(
            froz_ref.at[:, :, pl.ds(at, 512)], weights.at[k, :, core], wsem.at[k]
        )
        copy.start()
        fetches.append(copy)
    batch = lax.axis_index("dp")
    z_at, side_at = batch // 2, lax.rem(batch, 2)
    z_peers = [lax.rem(z_at + k, 4) for k in range(1, 4)]
    side_peer = 2 * z_at + 1 - side_at
    meet(others, [2 * z + side_at for z in z_peers] + [side_peer])

    def token_slice(peer):
        at = pl.multiple_of((peer // 4) * BLOCK, BLOCK)
        start_row = pl.multiple_of(lax.rem(peer, 2) * ROWS, ROWS)
        return tok_ref.at[pl.ds(start_row, ROWS), pl.ds(at, BLOCK)]

    gather(grad_ref, place(3, 0), None, up)
    gather(grad_ref, place(1, 0), None, down)
    gather(grad_ref, place(0, 1), None, across)
    for k, peer in enumerate(others):
        go(push(token_slice(peer), x_scr.at[me], tsend.at[k], trecv.at[me], peer))
    pltpu.make_async_copy(token_slice(me), x_scr.at[me], trecv.at[me]).start()
    for k, (dy, dx) in enumerate(ORDER):
        target = 2 * lax.rem(y_at + dy, 4) + lax.rem(x_at + dx, 2)
        at = pl.multiple_of((2 * target + 1 - core) * 512, 512)
        go(push(
            froz_ref.at[:, :, pl.ds(at, 512)], weights.at[k, :, core], fsend.at[k], frecv.at[k], partner
        ))

    inverse_blocks(local_param, cross_param, inv_ref, rot)

    jobs = []
    for k in range(4):
        c = lax.rem(chip + k, 4)
        for side in range(2):
            jobs.append((
                rot.at[c, pl.ds(side * HALF, HALF), :], local.at[chip, core],
                lsend.at[k, side], lrecv.at[chip], 2 * (2 * c + side) + core, me,
            ))
    for level in range(4):
        bit, pair = pair_place(me, level)
        for k in range(4):
            c = lax.rem(chip + k, 4)
            jobs.append((
                rot.at[4 + 4 * level + c], cross.at[level, pair // 2, lax.rem(pair, 2)],
                send.at[level, k], recv.at[level, pair // 2],
                2 * (c + 4 * bit) + lax.rem(pair, 2), me,
            ))
    gathered(place(3, 0))
    gather(grads.at[place(3, 0)], place(2, 0), 0, up)
    gathered(place(1, 0))
    gather(grads.at[place(1, 0)], place(2, 0), 1, down)
    for job in jobs:
        start_job(*job)
    gathered(place(0, 1))
    gather(grads.at[place(0, 1)], place(3, 1), None, up)
    gather(grads.at[place(0, 1)], place(1, 1), None, down)

    def forward_on(stage):
        if stage == 0:
            for q in range(CHIPS):
                arrived(local.at[q, core], lrecv.at[q])
            part = local.at[:, core]
        else:
            for q in range(4):
                arrived(cross.at[stage - 1, q, core], recv.at[stage - 1, q])
            part = cross.at[stage - 1, :, core]
        go(push(part, part, psend.at[stage], precv.at[stage], partner))

    def weight(k):
        return weights[k].reshape(1024, 512)

    def cotangent(slot, first=False):
        fetches[slot].wait()
        arrived(weights.at[slot, :, 1 - core], frecv.at[slot])
        for rows, total_ref in ((other_row, theirs), (row, mine)):
            value = dot(grads[slot, pl.ds(rows, ROWS), :], weight(slot), NT)
            if first:
                total_ref[...] = value
            else:
                total_ref[...] += value

    forward_on(0)
    forward_on(1)
    for peer in [me] + others:
        arrived(x_scr.at[peer], trecv.at[peer])
    gathered(place(0, 0))
    cotangent(place(0, 0), True)
    arrived(local.at[:, 1 - core], precv.at[0])
    lanes = lax.broadcasted_iota(jnp.int32, (ROWS, BLOCK), 1)
    for m in range(CHIPS):
        parts = []
        for side in range(2):
            high, low = split(jnp.concatenate([local[m, side]] * 2, axis=0))
            x = x_scr[2 * m + side]
            parts.append(dot(x, high, NT) + dot(x, low, NT))
        saved[0, m // 2, :, (m % 2) * BLOCK:(m % 2 + 1) * BLOCK] = jnp.where(
            lanes < HALF, parts[0], parts[1]
        )
    for level in range(4):
        if level < 3:
            forward_on(level + 2)
        if level == 0:
            gathered(place(2, 0), 0)
            gathered(place(2, 0), 1)
            gather(grads.at[place(2, 0)], place(2, 1), None, across)
            cotangent(place(0, 1))
            cotangent(place(3, 0))
        if level == 1:
            cotangent(place(1, 0))
        if level == 2:
            cotangent(place(2, 0))
        arrived(cross.at[level, :, 1 - core], precv.at[level + 1])
        outs = []
        for index in range(4):
            one, two = pairs_of(level, index)
            a = cross[level, one // 2, one % 2]
            b = cross[level, two // 2, two % 2]
            matrix = split(place_near(a, b) if level % 2 == 0 else place_far(a, b))
            mats[level, index, 0] = matrix[0]
            mats[level, index, 1] = matrix[1]
            outs.append(dot3(split(saved[level, index]), matrix))
        if level % 2 == 1:
            outs = regroup(outs)
        for index in range(4):
            if level < 3:
                saved[level + 1, index] = outs[index]
            else:
                rotated[:, index * 256:(index + 1) * 256] = outs[index].astype(BF16)
    for slot in (place(3, 1), place(1, 1), place(2, 1)):
        gathered(slot)
        cotangent(slot)
    swap = push(theirs, landed, psend.at[5], precv.at[5], partner)
    swap.start()
    swap.wait()
    rounded[...] = (mine[...] + landed[...]).astype(BF16)
    landing = rg.at[:, pl.ds(column, BLOCK)]
    for k, peer in enumerate(peers):
        source = pl.multiple_of((peer // 2) * BLOCK, BLOCK)
        go(push(rounded.at[:, pl.ds(source, BLOCK)], landing, rsend.at[k], rrecv.at[chip], peer))
    pltpu.make_async_copy(rounded.at[:, pl.ds(column, BLOCK)], landing, rrecv.at[chip]).start()
    landing = act.at[pl.ds(row, ROWS), pl.ds(column, BLOCK)]
    for k, peer in enumerate(peers):
        source = pl.multiple_of((peer // 2) * BLOCK, BLOCK)
        go(push(rotated.at[:, pl.ds(source, BLOCK)], landing, asend.at[k], arecv.at[chip], peer))
    pltpu.make_async_copy(rotated.at[:, pl.ds(column, BLOCK)], landing, arecv.at[chip]).start()

    def product(k, half):
        return dot(act[half * ROWS:(half + 1) * ROWS], weight(k))

    def ready(slot, value):
        sends_buf[slot] = value.astype(BF16)

    def give(slot, value, peer):
        ready(slot, value)
        go(push(sends_buf.at[slot], lands.at[slot], osend.at[slot], orecv.at[slot], peer))

    def take(slot):
        arrived(lands.at[slot], orecv.at[slot])
        return lands[slot].astype(F32)

    for peer in [me] + peers:
        at = pl.multiple_of((peer // 2) * BLOCK, BLOCK)
        arrived(rg.at[:, pl.ds(at, BLOCK)], rrecv.at[peer // 2])

    state = [rg[:, index * 256:(index + 1) * 256].astype(F32) for index in range(4)]
    state = regroup(state)
    swaps = []

    def send_back(level):
        swaps[3 - level].wait()
        cross_in[level] = cross_in[level] + grad_cross[level, core]
        slot = lax.rem(chip, 4)
        for k in range(4):
            q = lax.rem(chip + k, 4)
            job = (
                cross_in.at[level, q], own.at[4 + 4 * level + slot],
                msend.at[level, k], mrecv.at[level, slot],
                pair_owner(2 * q + core, level, chip // 4), me,
            )
            start_job(*job)
            jobs.append(job)

    for level in (3, 2, 1, 0):
        outs = []
        for index in range(4):
            grad = split(state[index])
            full = dot3(split(saved[level, index]), grad, TN)
            if level % 2 == 0:
                a, b = full[:BLOCK, :BLOCK], full[BLOCK:, BLOCK:]
            else:
                a, b = take_far(full)
            one, two = pairs_of(level, index)
            grad_cross[level, one % 2, one // 2] = a
            grad_cross[level, two % 2, two // 2] = b
            outs.append(dot3(grad, (mats[level, index, 0], mats[level, index, 1]), NT))
        state = regroup(outs) if level == 2 else outs
        copy = push(
            grad_cross.at[level, 1 - core], cross_in.at[level], bsend.at[level], brecv.at[level], partner
        )
        copy.start()
        swaps.append(copy)
        if level == 3:
            for peer in [me] + peers:
                at = pl.multiple_of((peer // 2) * BLOCK, BLOCK)
                arrived(act.at[pl.ds(row, ROWS), pl.ds(at, BLOCK)], arecv.at[peer // 2])
            part = act.at[pl.ds(row, ROWS), :]
            go(push(part, part, psend.at[6], precv.at[6], partner))
        else:
            send_back(level + 1)
    for m in range(CHIPS):
        grad = split(state[m // 2][:, (m % 2) * BLOCK:(m % 2 + 1) * BLOCK])
        for side in range(2):
            x = x_scr[2 * m + side]
            full = dot(grad[0], x, TN) + dot(grad[1], x, TN)
            grad_local[side, m] = full[side * HALF:(side + 1) * HALF]
    copy = push(grad_local.at[1 - core], local_in, bsend.at[4], brecv.at[4], partner)
    copy.start()
    swaps.append(copy)
    send_back(0)
    swaps[4].wait()
    local_in[...] = local_in[...] + grad_local[core]
    for k in range(CHIPS):
        q = lax.rem(chip + k, CHIPS)
        side = pl.multiple_of(lax.rem(chip, 2) * HALF, HALF)
        job = (
            local_in.at[q], own.at[chip // 2, pl.ds(side, HALF), :],
            nsend.at[k], nrecv.at[chip], 2 * q + core, me,
        )
        start_job(*job)
        jobs.append(job)
    arrived(act.at[pl.ds(other_row, ROWS), :], precv.at[6])
    for half in range(2):
        for k in range(3):
            ready(2 * k + half, product(k, half))
    for level in range(4):
        for c in range(4):
            arrived(own.at[4 + 4 * level + c], mrecv.at[level, c])
    for g in range(CHIPS):
        arrived(own.at[g // 2, pl.ds((g % 2) * HALF, HALF), :], nrecv.at[g])
    own_rows = pl.ds(pl.multiple_of(z_at * 32, 32), 32)
    for k, z in enumerate(z_peers):
        z_send[k] = own[:, pl.ds(pl.multiple_of(z * 32, 32), 32), :].astype(BF16)
        go(push(z_send.at[k], z_land.at[z_at], zsend.at[k], zrecv.at[z_at], 2 * z + side_at, "dp"))
    for half in range(2):
        for k, peer in ((0, up), (1, down), (2, across)):
            slot = 2 * k + half
            go(push(sends_buf.at[slot], lands.at[slot], osend.at[slot], orecv.at[slot], peer))
    give(8, product(4, 1), up)
    give(9, product(5, 0), down)
    value = own[:, own_rows, :]
    for z in z_peers:
        arrived(z_land.at[z], zrecv.at[z])
        value = value + z_land[z].astype(F32)
    z_sum[...] = value
    their_part = pl.ds(pl.multiple_of((1 - side_at) * 16, 16), 16)
    my_part = pl.ds(pl.multiple_of(side_at * 16, 16), 16)
    go(push(z_sum.at[:, their_part, :], side_land, zsend.at[3], zrecv.at[4], side_peer, "dp"))
    give(6, product(3, 0) + take(4), up)
    give(7, product(3, 1) + take(5), down)
    for half in range(2):
        give(12 + half, product(6, half) + (take(0 + half) + take(2 + half)), across)
    arrived(side_land, zrecv.at[4])
    my_rows = pl.ds(pl.multiple_of(z_at * 32 + side_at * 16, 16), 16)
    their_rows = pl.ds(pl.multiple_of(z_at * 32 + (1 - side_at) * 16, 16), 16)
    total_ref[:, my_rows, :] = z_sum[:, my_part, :] + side_land[...]
    mine_rows = total_ref.at[:, my_rows, :]
    go(push(mine_rows, mine_rows, zsend.at[4], zrecv.at[5], side_peer, "dp"))
    give(10, product(4, 0) + take(6), up)
    give(11, product(5, 1) + take(7), down)
    arrived(total_ref.at[:, their_rows, :], zrecv.at[5])
    both = total_ref.at[:, own_rows, :]
    for k, z in enumerate(z_peers):
        go(push(both, both, zsend.at[5 + k], zrecv.at[6 + z_at], 2 * z + side_at, "dp"))
    out_ref[0:ROWS] = product(7, 0) + (take(9) + take(12)) + take(10)
    out_ref[ROWS:] = product(7, 1) + (take(8) + take(13)) + take(11)
    for z in z_peers:
        arrived(total_ref.at[:, pl.ds(pl.multiple_of(z * 32, 32), 32), :], zrecv.at[6 + z])
    for at in range(20):
        matrix = total_ref[at].T if at < 4 else total_ref[at]
        inverse = split(inv_ref[at])
        left = dot3(inverse, split(matrix), TN)
        full = dot3(split(left), inverse, NT)
        pulled = -2.0 * (full - full.T)
        if at < 4:
            local_out[at] = pulled
        else:
            cross_out[(at - 4) // 4, at % 4] = pulled
    for copy in sends:
        copy.wait_send()
    for job in jobs:
        drain_job(*job)


def layer(tokens, frozen, grads, local_param, cross_param):
    return pl.pallas_call(
        layer_kernel,
        out_shape=(
            jax.ShapeDtypeStruct((512, 512), F32), jax.ShapeDtypeStruct((4, BLOCK, BLOCK), F32),
            jax.ShapeDtypeStruct((4, 4, BLOCK, BLOCK), F32),
        ),
        in_specs=[ANY, ANY, ANY, VMEM, VMEM],
        out_specs=(VMEM, VMEM, VMEM),
        scratch_shapes=[
            pltpu.VMEM((GROUP, ROWS, BLOCK), BF16), pltpu.VMEM((20, BLOCK, BLOCK), F32),
            pltpu.VMEM((4, 4, 2, BLOCK, BLOCK), F32), pltpu.VMEM((CHIPS, 2, HALF, BLOCK), F32),
            pltpu.VMEM((4, 4, 2, 256, 256), BF16), pltpu.VMEM((4, 4, ROWS, 256), F32),
            pltpu.VMEM((ROWS, 1024), BF16), pltpu.VMEM((512, 1024), BF16),
            pltpu.VMEM((CHIPS, CHIPS, 2, HALF, 512), BF16), pltpu.VMEM((CHIPS, 512, 512), BF16),
            pltpu.VMEM((14, ROWS, 512), BF16), pltpu.VMEM((14, ROWS, 512), BF16),
            pltpu.VMEM((ROWS, 1024), F32), pltpu.VMEM((ROWS, 1024), F32),
            pltpu.VMEM((ROWS, 1024), F32), pltpu.VMEM((ROWS, 1024), BF16),
            pltpu.VMEM((ROWS, 1024), BF16),
            pltpu.VMEM((4, 2, 4, BLOCK, BLOCK), F32), pltpu.VMEM((2, CHIPS, HALF, BLOCK), F32),
            pltpu.VMEM((4, 4, BLOCK, BLOCK), F32), pltpu.VMEM((CHIPS, HALF, BLOCK), F32),
            pltpu.VMEM((20, BLOCK, BLOCK), F32), pltpu.VMEM((20, BLOCK, BLOCK), F32),
            pltpu.VMEM((20, BLOCK, BLOCK), F32), pltpu.VMEM((3, 20, 32, BLOCK), BF16),
            pltpu.VMEM((4, 20, 32, BLOCK), BF16), pltpu.VMEM((20, 32, BLOCK), F32),
            pltpu.VMEM((20, 16, BLOCK), F32),
            DMA((GROUP,)), DMA((GROUP,)), DMA((CHIPS,)), DMA((CHIPS,)), DMA((CHIPS,)),
            DMA((4, 4)), DMA((4, 4)), DMA((4, 2)), DMA((CHIPS,)), DMA((7,)), DMA((7,)),
            DMA((CHIPS,)), DMA((CHIPS,)), DMA((9,)), DMA((9,)), DMA((14,)), DMA((14,)),
            DMA((CHIPS,)), DMA((CHIPS,)), DMA((5,)), DMA((5,)), DMA((4, 4)), DMA((4, 4)),
            DMA((CHIPS,)), DMA((CHIPS,)), DMA((8,)), DMA((10,)),
        ],
        compiler_params=params_of(0),
    )(tokens, frozen.reshape(CHIPS, HALF, 8192), grads, local_param, cross_param)


def body(tokens, frozen, local_param, cross_param, out_grad):
    return layer(tokens, frozen, out_grad, local_param, cross_param)


def solution(mesh):
    in_specs = (
        P("dp", "tensor"),
        P("tensor", None),
        P("tensor", None, None),
        P(None, "tensor", None, None),
        P("dp", "tensor"),
    )
    out_specs = (P("dp", "tensor"), P("tensor", None, None), P(None, "tensor", None, None))
    return jax.shard_map(body, mesh=mesh, in_specs=in_specs, out_specs=out_specs, check_vma=False)
```
